1024 devices in a mesh: dp: 16 (over y_hi, x, core), fsdp: 64 (over y_lo, z).
Axes of the slice: x: 4, y: 8 (y_hi: 2, y_lo: 4; y = y_hi * 4 + y_lo), z: 16, core: 2. Of those that a mesh axis runs over, the one named last changes fastest.
Arguments:
- inputs: bfloat16 [32768, 8192], P('dp', 'fsdp'), may hold values from -57 to 57
- out_grads: bfloat16 [32768, 28672], P('dp', 'fsdp'), may hold values from -57 to 57
- proj_in: bfloat16 [8192, 64], P('fsdp'), may hold values from -0.0625 to 0.0625
- proj_out: bfloat16 [28672, 64], P('fsdp'), may hold values from -0.03125 to 0.03125
- segment_ids: int32 [16, 2048], P('dp'), may hold values from 0 to 15, never falling along the last dimension, each value on 1 to 256 neighbouring positions
- sketch: float32 [4096, 512], P('fsdp'), may hold values from -0.09375 to 0.09375
Outputs:
- new_sketch: float32 [4096, 512], P('fsdp')
- precond: float32 [256, 512], P('dp')
The draws below stay inside these ranges and needn't reach their ends.
Inputs may be any that keep to these rules, and one draw needn't show every extreme that they name: `segment_ids`: in each group the tokens, in order, form 16 examples of 1 to 256 tokens, and some example has exactly 256.
All inputs are finite; a program needn't handle non-finite values.
Results may differ from the reference program's by a relative error of at most 0.0003.
Values sent between devices are 32-bit elements; how exact they have to be, the bound alone decides.
No kernel may reach another device: no remote copies, remote signals or barrier semaphores. Data moves between devices by JAX's collectives and lax.ppermute only.
A program may use at most 32 MiB of HBM per device.

```python
import math
import jax
import jax.numpy as jnp
import numpy as np
from jax import lax

D = 8192
FF = 28672
KP = 64
RANK = 512
TOK_GROUP = 2048
EX_GROUP = 16
MOST = 256
FEAT = 4096
GROUPS = 16
TOKENS = 32768
EXAMPLES = 256


def scale_values(key, base_values, row_total, col_total):
    row_key, col_key = jax.random.split(key)
    row_position = jnp.arange(row_total, dtype=jnp.float32)[:, None] / row_total
    col_position = jnp.arange(col_total, dtype=jnp.float32)[None, :] / col_total
    row_factor = jnp.exp(row_position * math.log(3.0) + jax.random.uniform(row_key, (row_total, 1), jnp.float32, 0.0, math.log(10.0))) / 8.0
    col_factor = jnp.exp(col_position * math.log(3.0) + jax.random.uniform(col_key, (1, col_total), jnp.float32, 0.0, math.log(10.0))) / 8.0
    return base_values * row_factor * col_factor


def draw_inputs(key, part):
    key = jax.random.fold_in(key, 11)
    base_key = jax.random.fold_in(key, 0)
    scale_key = jax.random.fold_in(key, 2)
    base_values = jnp.clip(jax.random.normal(base_key, (TOKENS, D), jnp.float32), -4.0, 4.0)
    return scale_values(scale_key, base_values, TOKENS, D).astype(jnp.bfloat16)


def draw_out_grads(key, part):
    key = jax.random.fold_in(key, 23)
    base_key = jax.random.fold_in(key, 0)
    scale_key = jax.random.fold_in(key, 2)
    base_values = jnp.clip(jax.random.normal(base_key, (TOKENS, FF), jnp.float32), -4.0, 4.0)
    return scale_values(scale_key, base_values, TOKENS, FF).astype(jnp.bfloat16)


def levels(own_key, dims, cuts, least, top_value):
    gain = 1.0
    for axis_at, parts in cuts:
        draws = jax.random.uniform(jax.random.fold_in(jax.random.fold_in(own_key, 6), axis_at), (parts,), jnp.float32, least / len(cuts), top_value / len(cuts))
        gain = gain * jnp.repeat(jnp.exp(draws), dims[axis_at] // parts).reshape((-1,) + (1,) * (len(dims) - 1 - axis_at))
    return gain


def split_up(count, total, reach, slope):
    loads = [(1 << 20) // math.isqrt(grade ** slope) + 1 for grade in range(2, count + 1)]
    spare, holding = total - reach - (count - 1), [1] * (count - 1)
    while spare > 0:
        free = [i for i in range(count - 1) if holding[i] < reach]
        whole, budget = sum([loads[i] for i in free]), spare
        for i in free:
            more = min(reach - holding[i], max(1, budget * loads[i] // whole), spare)
            holding[i] = holding[i] + more
            spare = spare - more
    return np.array([reach] + holding)


def uneven_parts(rng, number_of, total, reach, slope):
    if number_of == 2:
        one = jax.random.randint(rng, (), max(1, total - reach), min(reach, total - 1) + 1)
        return jnp.stack([one, total - one])
    tallies = jnp.asarray(split_up(number_of, total, reach, slope), jnp.int32)
    pairs = (number_of - 1) // 2
    giver, sink = tallies[1:1 + 2 * pairs:2], tallies[2:2 + 2 * pairs:2]
    margin = jnp.minimum(giver - 1, reach - sink)
    moved = jax.random.randint(jax.random.fold_in(rng, 1), (pairs,), 0, 1 << 20) % (margin + 1)
    tallies = tallies.at[1:1 + 2 * pairs:2].set(giver - moved).at[2:2 + 2 * pairs:2].set(sink + moved)
    return tallies[jax.random.permutation(jax.random.fold_in(rng, 2), number_of)]


def noise(key, extent, deviation, most, cuts=(), held_as=jnp.bfloat16):
    values = jax.random.normal(key, extent, jnp.float32) * deviation
    if len(cuts) > 0:
        values = levels(key, extent, cuts, -0.22, 0.18) * values
    return jnp.clip(values, min=-most, max=most).astype(held_as)


def setup_inputs(seed: int = 0) -> dict:
    streams_of = jax.random.split(jax.random.key(seed), 7)
    return {
        "inputs": draw_inputs(jax.random.fold_in(streams_of[6], 71), 0),
        "out_grads": draw_out_grads(jax.random.fold_in(streams_of[6], 71), 0),
        "proj_in": noise(streams_of[2], (D, KP), D ** -0.5, 0.0625, ((0, 64),)),
        "proj_out": noise(streams_of[3], (FF, KP), FF ** -0.5, 0.03125, ((0, 64),)),
        "segment_ids": jax.vmap(lambda own: jnp.searchsorted(jnp.cumsum(uneven_parts(own, EX_GROUP, TOK_GROUP, MOST, 1)), jnp.arange(TOK_GROUP), side="right"))(jax.random.split(streams_of[4], GROUPS)).reshape((GROUPS, TOK_GROUP)).astype(jnp.int32),
        "sketch": noise(streams_of[5], (FEAT, RANK), (1.0 / KP), 0.09375, ((0, 64),), jnp.float32),
    }


rate_gain = 16.0
epsilon = 1e-06

def group_features(block):
    inputs_grp, grads_grp, segment_row, proj_in, proj_out = block
    in_part = jnp.dot(inputs_grp.astype(jnp.float32), proj_in.astype(jnp.float32), preferred_element_type=jnp.float32)
    out_part = jnp.dot(grads_grp.astype(jnp.float32), proj_out.astype(jnp.float32), preferred_element_type=jnp.float32)
    onehot = (segment_row[:, None] == jnp.arange(EX_GROUP, dtype=jnp.int32)[None, :]).astype(jnp.float32)
    counts = lax.optimization_barrier(jnp.sum(onehot, axis=0))
    weighted = (onehot[:, :, None] * in_part[:, None, :]).reshape(TOK_GROUP, EX_GROUP * KP)
    summed = jnp.einsum('tm,tj->mj', weighted, out_part, precision=lax.Precision.HIGHEST)
    return summed.reshape(EX_GROUP, FEAT) / counts[:, None]

def reference(inputs, out_grads, proj_in, proj_out, segment_ids, sketch):
    inputs_grp = inputs.reshape(GROUPS, TOK_GROUP, D)
    grads_grp = out_grads.reshape(GROUPS, TOK_GROUP, FF)
    features = lax.map(lambda pair: group_features((pair[0], pair[1], pair[2], proj_in, proj_out)), (inputs_grp, grads_grp, segment_ids))
    features = features.reshape(EXAMPLES, FEAT)
    high = lax.Precision.HIGHEST
    scores = jnp.dot(features, sketch, precision=high)
    total_sq = jnp.sum(features * features)
    moment = jnp.dot(features.T, scores, precision=high)
    fresh_sketch = sketch + rate_gain / (total_sq + epsilon) * moment
    gram_matrix = jnp.dot(fresh_sketch.T, fresh_sketch, precision=high)
    lower_factor = jnp.linalg.cholesky(gram_matrix)
    new_sketch = jax.scipy.linalg.solve_triangular(lower_factor, fresh_sketch.T, lower=True).T
    coefs = jnp.dot(features, new_sketch, precision=high)
    spectrum_mean = lax.optimization_barrier(jnp.sum(coefs * coefs, axis=0)) / EXAMPLES
    precond = coefs / jnp.sqrt(spectrum_mean + epsilon)[None, :]
    return (new_sketch, precond)
```

```python
import functools

import jax
import jax.numpy as jnp
from jax import lax
from jax.experimental import pallas as pl
from jax.experimental.pallas import tpu as pltpu
from jax.sharding import Mesh
from jax.sharding import PartitionSpec as P

HI = lax.Precision.HIGHEST
EX_GROUP = 16
DP = ("yh", "x", "c")
XC = ("x", "c")
FS = ("yl", "z")


def mm(a, b, dims, prec=HI):
    return lax.dot_general(a, b, (dims, ((), ())), precision=prec, preferred_element_type=jnp.float32)

def factor_block(d_ref, w_ref):
    nb = 128
    full = (8, nb)
    xs = [d_ref[8 * v: 8 * v + 8, :] for v in range(nb // 8)]
    ws = [w_ref[8 * v: 8 * v + 8, :] for v in range(nb // 8)]
    for p in range(nb // 8):
        base = 8 * p
        xr = [jnp.broadcast_to(xs[p][i:i + 1, :], full) for i in range(8)]
        wr = [jnp.broadcast_to(ws[p][i:i + 1, :], full) for i in range(8)]
        s = [[jnp.broadcast_to(xr[i][:, base + j:base + j + 1], full) for j in range(i + 1)] for i in range(8)]
        m = [[None] * 8 for _ in range(8)]
        inv = [None] * 8
        for k in range(8):
            inv[k] = 1.0 / s[k][k]
            for i in range(k + 1, 8):
                m[i][k] = s[i][k] * inv[k]
                for j in range(k + 1, i + 1):
                    s[i][j] = s[i][j] - m[i][k] * s[j][k]
        for i in range(8):
            for k in range(i):
                xr[i] = xr[i] - m[i][k] * xr[k]
                wr[i] = wr[i] - m[i][k] * wr[k]
        for i in range(8):
            w_ref[base + i: base + i + 1, :] = (wr[i] * lax.rsqrt(s[i][i]))[0:1, :]
        if p == nb // 8 - 1:
            break
        xv = [xr[i] * inv[i] for i in range(8)]
        wv = [wr[i] * inv[i] for i in range(8)]
        for i in range(7, -1, -1):
            for k in range(i + 1, 8):
                xv[i] = xv[i] - m[k][i] * xv[k]
                wv[i] = wv[i] - m[k][i] * wv[k]
        for q in range(p + 1, nb // 8):
            cols = [jnp.broadcast_to(xs[q][:, base + i:base + i + 1], full) for i in range(8)]
            for i in range(8):
                xs[q] = xs[q] - cols[i] * xv[i]
                ws[q] = ws[q] - cols[i] * wv[i]

def products_kernel(at_ref, tiles_ref, sketch_ref, gram_ref, sums_ref, features_ref):
    groups, half, lanes = tiles_ref.shape
    width = lanes // 2
    for g in range(groups):
        to = ((g % (groups // 2)) * 2 + g // (groups // 2)) * 2 * half
        tile = tiles_ref[g]
        features_ref[to:to + half, :] = tile[:, :width]
        features_ref[to + half:to + 2 * half, :] = tile[:, width:]
    rows = 4 * half
    features = features_ref[...]
    own = features_ref[pl.ds(pl.multiple_of(at_ref[0] * rows, rows), rows), :]
    inner = mm(own, features, ((1,), (1,)))
    scores = mm(own, sketch_ref[...], ((1,), (0,)))
    at = 0
    for part in (inner, scores, gram_ref[...]):
        for o in range(0, part.shape[1], lanes):
            sums_ref[at:at + part.shape[0], :] = part[:, o:o + lanes]
            at += part.shape[0]
    sums_ref[at:, :] = jnp.zeros((sums_ref.shape[0] - at, lanes), jnp.float32)


def products(block, tiles, sketch, gram_rows):
    vmem = pl.BlockSpec(memory_space=pltpu.VMEM)
    return pl.pallas_call(
        products_kernel,
        out_shape=(jax.ShapeDtypeStruct((512, 128), jnp.float32), jax.ShapeDtypeStruct((256, 64), jnp.float32)),
        in_specs=[pl.BlockSpec(memory_space=pltpu.SMEM), vmem, vmem, vmem],
        out_specs=(vmem, vmem),
        compiler_params=pltpu.CompilerParams(vmem_limit_bytes=24 * 1024 * 1024),
        name="products",
    )(block, tiles, sketch, gram_rows)


def finish_kernel(at_ref, sums_ref, f_ref, s_ref, ns_ref, co_ref, a_ref, x_ref, k_ref, p_ref, d_ref, w_ref):
    n = a_ref.shape[0]
    own, e = f_ref.shape[1], f_ref.shape[0]
    blocks = sums_ref.shape[0]
    rows, cut = e // blocks, n // blocks
    for b in range(blocks):
        at = 0
        for to, height in ((k_ref, rows), (p_ref, rows), (a_ref, cut)):
            for o in range(0, to.shape[1], 128):
                to[b * height:(b + 1) * height, o:o + 128] = sums_ref[b, at:at + height, :]
                at += height
    k = k_ref[...]
    p = p_ref[...]
    er = lax.broadcasted_iota(jnp.int32, (e, e), 0)
    ec = lax.broadcasted_iota(jnp.int32, (e, e), 1)
    total_sq = jnp.sum(jnp.sum(jnp.where(er == ec, k, 0.0), axis=0, keepdims=True), axis=1, keepdims=True)
    c = 16.0 / (total_sq + 1e-6)
    q = p + mm(k * c, p, ((1,), (0,)))
    x_ref[:own, :] = s_ref[...] + mm(f_ref[...] * c, p, ((0,), (0,)))
    x_ref[own:, :] = q
    a_ref[...] = a_ref[...] + mm(p * c, p + q, ((0,), (0,)))
    colid = lax.broadcasted_iota(jnp.int32, (128, n), 1)
    ri = lax.broadcasted_iota(jnp.int32, (128, 128), 0)
    ci = lax.broadcasted_iota(jnp.int32, (128, 128), 1)

    def step(b, carry):
        o = pl.multiple_of(b * 128, 128)
        d_ref[...] = a_ref[pl.ds(o, 128), pl.ds(o, 128)]
        w_ref[...] = jnp.where(ri == ci, 1.0, 0.0)
        factor_block(d_ref, w_ref)
        w = w_ref[...]
        r = mm(w, a_ref[pl.ds(o, 128), :], ((1,), (0,)))
        r = jnp.where(colid >= o + 128, r, 0.0)
        y = mm(x_ref[:, pl.ds(o, 128)], w, ((1,), (1,)))
        x_ref[...] = x_ref[...] - mm(y, r, ((1,), (0,)))
        x_ref[:, pl.ds(o, 128)] = y
        a_ref[...] = a_ref[...] - mm(r, r, ((0,), (0,)))
        return carry

    lax.fori_loop(0, n // 128, step, 0)
    ns_ref[...] = x_ref[:own, :]
    coefs = x_ref[own:, :]
    mean = jnp.sum(coefs * coefs, axis=0, keepdims=True) / e
    mine = x_ref[pl.ds(pl.multiple_of(own + at_ref[0] * EX_GROUP, EX_GROUP), EX_GROUP), :]
    co_ref[...] = mine / jnp.sqrt(mean + 1e-6)


def finish(at, sums, f, s):
    n, own, e = s.shape[1], s.shape[0], f.shape[0]
    vmem = pl.BlockSpec(memory_space=pltpu.VMEM)
    return pl.pallas_call(
        finish_kernel,
        out_shape=(jax.ShapeDtypeStruct((own, n), jnp.float32), jax.ShapeDtypeStruct((EX_GROUP, n), jnp.float32)),
        in_specs=[pl.BlockSpec(memory_space=pltpu.SMEM), vmem, vmem, vmem],
        out_specs=(vmem, vmem),
        scratch_shapes=[
            pltpu.VMEM((n, n), jnp.float32),
            pltpu.VMEM((own + e, n), jnp.float32),
            pltpu.VMEM((e, e), jnp.float32),
            pltpu.VMEM((e, n), jnp.float32),
            pltpu.VMEM((128, 128), jnp.float32),
            pltpu.VMEM((128, 128), jnp.float32),
        ],
        compiler_params=pltpu.CompilerParams(vmem_limit_bytes=40 * 1024 * 1024),
        name="finish",
    )(at, sums, f, s)


def exchange(x, axes):
    return lax.all_to_all(x, axes, 0, 0, tiled=True)


def spread(x, axes):
    return exchange(jnp.broadcast_to(x[None], (lax.axis_size(axes),) + x.shape), axes)


def outer_kernel(part_ref, seg_ref, out_ref):
    both = jnp.sum(part_ref[...], axis=0)
    tokens, width = both.shape[0], both.shape[1] // 2
    half = EX_GROUP // 2
    left = both[:, :width]
    col = lax.broadcasted_iota(jnp.int32, (width, width * half), 1)
    row = lax.broadcasted_iota(jnp.int32, (width, width * half), 0)
    repeat = jnp.where(col // half == row, 1.0, 0.0)
    wide = mm(left, repeat, ((1,), (0,)))
    slot = lax.broadcasted_iota(jnp.int32, (tokens, width * half), 1) % half
    seg = seg_ref[...]
    low = jnp.where(slot == seg, wide, 0.0)
    high = jnp.where(slot + half == seg, wide, 0.0)
    lane = lax.broadcasted_iota(jnp.int32, both.shape, 1)
    right = jnp.concatenate([both[:, width:], both[:, width:]], axis=1)
    right_low = jnp.where(lane < width, right, 0.0)
    right_high = jnp.where(lane < width, 0.0, right)
    out = mm(low, right_low, ((0,), (0,))) + mm(high, right_high, ((0,), (0,)))
    out_ref[...] = out.reshape(out_ref.shape)


def outer(parts, seg):
    width = parts.shape[2] // 2
    return pl.pallas_call(
        outer_kernel,
        out_shape=jax.ShapeDtypeStruct((width, EX_GROUP // 2, 2 * width), jnp.float32),
        in_specs=[pl.BlockSpec(memory_space=pltpu.VMEM)] * 2,
        out_specs=pl.BlockSpec(memory_space=pltpu.VMEM),
        compiler_params=pltpu.CompilerParams(vmem_limit_bytes=24 * 1024 * 1024),
        name="outer",
    )(parts, seg)


def per_device(inputs, out_grads, proj_in, proj_out, segment_ids, sketch):
    owners = lax.axis_size(FS)
    blocks = lax.axis_size(XC)
    tokens = inputs.shape[0]
    width = proj_in.shape[1]
    rank = sketch.shape[1]
    half = EX_GROUP // 2
    own_tokens = tokens // owners
    place = lax.axis_index(FS)
    block = lax.axis_index(XC)

    cut = rank // blocks
    gram_rows = mm(lax.dynamic_slice_in_dim(sketch, block * cut, cut, 1), sketch, ((0,), (0,)))

    segments = segment_ids[0]
    onehot = segments[:, None] == jnp.arange(EX_GROUP, dtype=jnp.int32)[None, :]
    counts = jnp.sum(onehot.astype(jnp.float32), axis=0)
    count_tile = jnp.repeat(counts.reshape(2, half).T, width, axis=1)
    own_segments = lax.dynamic_slice_in_dim(segments, place * own_tokens, own_tokens, 0)[:, None]

    projected = jnp.concatenate(
        [
            jnp.dot(inputs, proj_in, preferred_element_type=jnp.float32),
            jnp.dot(out_grads, proj_out, preferred_element_type=jnp.float32),
        ],
        axis=1,
    )
    parts = exchange(projected.reshape(owners, own_tokens, 2 * width), FS)
    partial_features = outer(parts, own_segments)
    tile = jnp.sum(exchange(partial_features, FS), axis=0) / count_tile
    tiles = spread(tile, DP)
    sums, features = products(block[None], tiles, sketch, gram_rows)
    chunk = jnp.sum(exchange(sums.reshape(owners, -1, 128), FS), axis=0)
    sums = spread(chunk, FS).reshape(sums.shape)[: 2 * EX_GROUP * 6 + cut * 4]
    sums = spread(sums, XC)
    at = block * 2 + lax.axis_index("yh")
    return finish(at[None], sums, features, sketch)


def solution(mesh):
    fine = Mesh(mesh.devices.reshape(2, 4, 2, 4, 16), ("yh", "x", "c", "yl", "z"))
    return jax.shard_map(
        per_device,
        mesh=fine,
        in_specs=(P(DP, FS), P(DP, FS), P(FS, None), P(FS, None), P(DP, None), P(FS, None)),
        out_specs=(P(FS, None), P(DP, None)),
        check_vma=False,
    )
```

```python
import functools

import jax
import jax.numpy as jnp
from jax import lax
from jax.experimental import pallas as pl
from jax.experimental.pallas import tpu as pltpu
from jax.sharding import Mesh
from jax.sharding import PartitionSpec as P

HI = lax.Precision.HIGHEST
EX_GROUP = 16
DP = ("yh", "x", "c")
XC = ("x", "c")
FS = ("yl", "z")
GRAM_HOPS = (("yl", 1), ("z", 1), ("yl", 2), ("z", 2), ("z", 4), ("z", 8))


def mm(a, b, dims, prec=HI):
    return lax.dot_general(a, b, (dims, ((), ())), precision=prec, preferred_element_type=jnp.float32)

def factor_block(d_ref, w_ref):
    nb = 128
    full = (8, nb)
    xs = [d_ref[8 * v: 8 * v + 8, :] for v in range(nb // 8)]
    ws = [w_ref[8 * v: 8 * v + 8, :] for v in range(nb // 8)]
    for p in range(nb // 8):
        base = 8 * p
        xr = [jnp.broadcast_to(xs[p][i:i + 1, :], full) for i in range(8)]
        wr = [jnp.broadcast_to(ws[p][i:i + 1, :], full) for i in range(8)]
        s = [[jnp.broadcast_to(xr[i][:, base + j:base + j + 1], full) for j in range(i + 1)] for i in range(8)]
        m = [[None] * 8 for _ in range(8)]
        inv = [None] * 8
        for k in range(8):
            inv[k] = 1.0 / s[k][k]
            for i in range(k + 1, 8):
                m[i][k] = s[i][k] * inv[k]
                for j in range(k + 1, i + 1):
                    s[i][j] = s[i][j] - m[i][k] * s[j][k]
        for i in range(8):
            for k in range(i):
                xr[i] = xr[i] - m[i][k] * xr[k]
                wr[i] = wr[i] - m[i][k] * wr[k]
        for i in range(8):
            w_ref[base + i: base + i + 1, :] = (wr[i] * lax.rsqrt(s[i][i]))[0:1, :]
        if p == nb // 8 - 1:
            break
        xv = [xr[i] * inv[i] for i in range(8)]
        wv = [wr[i] * inv[i] for i in range(8)]
        for i in range(7, -1, -1):
            for k in range(i + 1, 8):
                xv[i] = xv[i] - m[k][i] * xv[k]
                wv[i] = wv[i] - m[k][i] * wv[k]
        for q in range(p + 1, nb // 8):
            cols = [jnp.broadcast_to(xs[q][:, base + i:base + i + 1], full) for i in range(8)]
            for i in range(8):
                xs[q] = xs[q] - cols[i] * xv[i]
                ws[q] = ws[q] - cols[i] * wv[i]

def products_kernel(at_ref, tiles_ref, sketch_ref, sums_ref, features_ref):
    groups, half, lanes = tiles_ref.shape
    width = lanes // 2
    for g in range(groups):
        to = ((g % (groups // 2)) * 2 + g // (groups // 2)) * 2 * half
        tile = tiles_ref[g]
        features_ref[to:to + half, :] = tile[:, :width]
        features_ref[to + half:to + 2 * half, :] = tile[:, width:]
    rows = 4 * half
    features = features_ref[...]
    own = features_ref[pl.ds(pl.multiple_of(at_ref[0] * rows, rows), rows), :]
    inner = mm(own, features, ((1,), (1,)))
    scores = mm(own, sketch_ref[...], ((1,), (0,)))
    at = 0
    for part in (inner, scores):
        for o in range(0, part.shape[1], lanes):
            sums_ref[at:at + part.shape[0], :] = part[:, o:o + lanes]
            at += part.shape[0]
    sums_ref[at:, :] = jnp.zeros((sums_ref.shape[0] - at, lanes), jnp.float32)


def products(block, tiles, sketch):
    vmem = pl.BlockSpec(memory_space=pltpu.VMEM)
    return pl.pallas_call(
        products_kernel,
        out_shape=(jax.ShapeDtypeStruct((256, 128), jnp.float32), jax.ShapeDtypeStruct((256, 64), jnp.float32)),
        in_specs=[pl.BlockSpec(memory_space=pltpu.SMEM), vmem, vmem],
        out_specs=(vmem, vmem),
        compiler_params=pltpu.CompilerParams(vmem_limit_bytes=24 * 1024 * 1024),
        name="products",
    )(block, tiles, sketch)


def finish_kernel(at_ref, sums_ref, sums2_ref, gram_ref, gram2_ref, f_ref, s_ref, ns_ref, co_ref, a_ref, x_ref, k_ref, p_ref, d_ref, w_ref):
    n = a_ref.shape[0]
    own, e = f_ref.shape[1], f_ref.shape[0]
    across = sums_ref.shape[0]
    rows, cut = e // (2 * across), n // (2 * across)
    for c in range(2):
        core = at_ref[1] if c == 0 else 1 - at_ref[1]
        sums, gram = (sums_ref, gram_ref) if c == 0 else (sums2_ref, gram2_ref)
        for b in range(across):
            at = 0
            for to in (k_ref, p_ref):
                for o in range(0, to.shape[1], 128):
                    to[pl.ds(pl.multiple_of((2 * b + core) * rows, rows), rows), o:o + 128] = sums[b, at:at + rows, :]
                    at += rows
            there = lax.rem(at_ref[2] + across - b, across)
            a_ref[pl.ds(pl.multiple_of((2 * there + core) * cut, cut), cut), :] = gram[b]
    k = k_ref[...]
    p = p_ref[...]
    er = lax.broadcasted_iota(jnp.int32, (e, e), 0)
    ec = lax.broadcasted_iota(jnp.int32, (e, e), 1)
    total_sq = jnp.sum(jnp.sum(jnp.where(er == ec, k, 0.0), axis=0, keepdims=True), axis=1, keepdims=True)
    c = 16.0 / (total_sq + 1e-6)
    q = p + mm(k * c, p, ((1,), (0,)))
    x_ref[:own, :] = s_ref[...] + mm(f_ref[...] * c, p, ((0,), (0,)))
    x_ref[own:, :] = q
    a_ref[...] = a_ref[...] + mm(p * c, p + q, ((0,), (0,)))
    colid = lax.broadcasted_iota(jnp.int32, (128, n), 1)
    ri = lax.broadcasted_iota(jnp.int32, (128, 128), 0)
    ci = lax.broadcasted_iota(jnp.int32, (128, 128), 1)

    def step(b, carry):
        o = pl.multiple_of(b * 128, 128)
        d_ref[...] = a_ref[pl.ds(o, 128), pl.ds(o, 128)]
        w_ref[...] = jnp.where(ri == ci, 1.0, 0.0)
        factor_block(d_ref, w_ref)
        w = w_ref[...]
        r = mm(w, a_ref[pl.ds(o, 128), :], ((1,), (0,)))
        r = jnp.where(colid >= o + 128, r, 0.0)
        y = mm(x_ref[:, pl.ds(o, 128)], w, ((1,), (1,)))
        x_ref[...] = x_ref[...] - mm(y, r, ((1,), (0,)))
        x_ref[:, pl.ds(o, 128)] = y
        a_ref[...] = a_ref[...] - mm(r, r, ((0,), (0,)))
        return carry

    lax.fori_loop(0, n // 128, step, 0)
    ns_ref[...] = x_ref[:own, :]
    coefs = x_ref[own:, :]
    mean = jnp.sum(coefs * coefs, axis=0, keepdims=True) / e
    mine = x_ref[pl.ds(pl.multiple_of(own + at_ref[0] * EX_GROUP, EX_GROUP), EX_GROUP), :]
    co_ref[...] = mine / jnp.sqrt(mean + 1e-6)


def finish(at, sums, sums2, gram, gram2, f, s):
    n, own, e = s.shape[1], s.shape[0], f.shape[0]
    vmem = pl.BlockSpec(memory_space=pltpu.VMEM)
    return pl.pallas_call(
        finish_kernel,
        out_shape=(jax.ShapeDtypeStruct((own, n), jnp.float32), jax.ShapeDtypeStruct((EX_GROUP, n), jnp.float32)),
        in_specs=[pl.BlockSpec(memory_space=pltpu.SMEM)] + [vmem] * 6,
        out_specs=(vmem, vmem),
        scratch_shapes=[
            pltpu.VMEM((n, n), jnp.float32),
            pltpu.VMEM((own + e, n), jnp.float32),
            pltpu.VMEM((e, e), jnp.float32),
            pltpu.VMEM((e, n), jnp.float32),
            pltpu.VMEM((128, 128), jnp.float32),
            pltpu.VMEM((128, 128), jnp.float32),
        ],
        compiler_params=pltpu.CompilerParams(vmem_limit_bytes=40 * 1024 * 1024),
        name="finish",
    )(at, sums, sums2, gram, gram2, f, s)


def exchange(x, axes):
    return lax.all_to_all(x, axes, 0, 0, tiled=True)


def spread(x, axes):
    return exchange(jnp.broadcast_to(x[None], (lax.axis_size(axes),) + x.shape), axes)


def swap(x, axis, bit):
    return lax.ppermute(x, axis, [(i, i ^ bit) for i in range(lax.axis_size(axis))])


def outer_kernel(part_ref, seg_ref, out_ref):
    both = jnp.sum(part_ref[...], axis=0)
    tokens, width = both.shape[0], both.shape[1] // 2
    half = EX_GROUP // 2
    left = both[:, :width]
    col = lax.broadcasted_iota(jnp.int32, (width, width * half), 1)
    row = lax.broadcasted_iota(jnp.int32, (width, width * half), 0)
    repeat = jnp.where(col // half == row, 1.0, 0.0)
    wide = mm(left, repeat, ((1,), (0,)))
    slot = lax.broadcasted_iota(jnp.int32, (tokens, width * half), 1) % half
    seg = seg_ref[...]
    low = jnp.where(slot == seg, wide, 0.0)
    high = jnp.where(slot + half == seg, wide, 0.0)
    lane = lax.broadcasted_iota(jnp.int32, both.shape, 1)
    right = jnp.concatenate([both[:, width:], both[:, width:]], axis=1)
    right_low = jnp.where(lane < width, right, 0.0)
    right_high = jnp.where(lane < width, 0.0, right)
    out = mm(low, right_low, ((0,), (0,))) + mm(high, right_high, ((0,), (0,)))
    out_ref[...] = out.reshape(out_ref.shape)


def outer(parts, seg):
    width = parts.shape[2] // 2
    return pl.pallas_call(
        outer_kernel,
        out_shape=jax.ShapeDtypeStruct((width, EX_GROUP // 2, 2 * width), jnp.float32),
        in_specs=[pl.BlockSpec(memory_space=pltpu.VMEM)] * 2,
        out_specs=pl.BlockSpec(memory_space=pltpu.VMEM),
        compiler_params=pltpu.CompilerParams(vmem_limit_bytes=24 * 1024 * 1024),
        name="outer",
    )(parts, seg)


def per_device(inputs, out_grads, proj_in, proj_out, segment_ids, sketch):
    owners = lax.axis_size(FS)
    blocks = lax.axis_size(XC)
    tokens = inputs.shape[0]
    width = proj_in.shape[1]
    rank = sketch.shape[1]
    half = EX_GROUP // 2
    own_tokens = tokens // owners
    place = lax.axis_index(FS)
    block = lax.axis_index(XC)

    segments = segment_ids[0]
    onehot = segments[:, None] == jnp.arange(EX_GROUP, dtype=jnp.int32)[None, :]
    counts = jnp.sum(onehot.astype(jnp.float32), axis=0)
    count_tile = jnp.repeat(counts.reshape(2, half).T, width, axis=1)
    own_segments = lax.dynamic_slice_in_dim(segments, place * own_tokens, own_tokens, 0)[:, None]

    projected = jnp.concatenate(
        [
            jnp.dot(inputs, proj_in, preferred_element_type=jnp.float32),
            jnp.dot(out_grads, proj_out, preferred_element_type=jnp.float32),
        ],
        axis=1,
    )
    cut = rank // blocks
    sketch_cols = lax.dynamic_slice_in_dim(sketch, block * cut, cut, 1)
    sketch_cols, projected = lax.optimization_barrier((sketch_cols, projected))
    gram = mm(sketch_cols, sketch, ((0,), (0,)))
    for axis, bit in GRAM_HOPS[:3]:
        gram = gram + swap(gram, axis, bit)
    parts = exchange(projected.reshape(4, -1, 2 * width), "yl")
    parts, gram = lax.optimization_barrier((parts, gram))
    for axis, bit in GRAM_HOPS[3:5]:
        gram = gram + swap(gram, axis, bit)
    parts = exchange(jnp.sum(parts, axis=0).reshape(-1, own_tokens, 2 * width), "z")
    parts, gram = lax.optimization_barrier((parts, gram))
    for axis, bit in GRAM_HOPS[5:]:
        gram = gram + swap(gram, axis, bit)
    partial_features = exchange(outer(parts, own_segments), FS)
    partial_features, gram = lax.optimization_barrier((partial_features, gram))
    tile = jnp.sum(partial_features, axis=0) / count_tile
    tiles = spread(tile, DP)
    features_sums = products(block[None], tiles, sketch)
    sums, features = features_sums
    around = lax.axis_size("x")
    gram = jnp.stack([gram] + [lax.ppermute(gram, "x", [(i, (i + s) % around) for i in range(around)]) for s in range(1, around)])
    sums = exchange(sums.reshape(owners, -1, 128), FS)
    sums, gram = lax.optimization_barrier((sums, gram))
    other_gram = swap(gram, "c", 1)
    sums = spread(jnp.sum(sums, axis=0), FS)
    sums, other_gram = lax.optimization_barrier((sums, other_gram))
    sums = spread(sums.reshape(-1, 128)[: 2 * EX_GROUP * 6], "x")
    other_sums = swap(sums, "c", 1)
    at = jnp.stack([block * 2 + lax.axis_index("yh"), lax.axis_index("c"), lax.axis_index("x")])
    return finish(at, sums, other_sums, gram, other_gram, features, sketch)


def solution(mesh):
    fine = Mesh(mesh.devices.reshape(2, 4, 2, 4, 16), ("yh", "x", "c", "yl", "z"))
    return jax.shard_map(
        per_device,
        mesh=fine,
        in_specs=(P(DP, FS), P(DP, FS), P(FS, None), P(FS, None), P(DP, None), P(FS, None)),
        out_specs=(P(FS, None), P(DP, None)),
        check_vma=False,
    )
```

```python
import functools

import jax
import jax.numpy as jnp
from jax import lax
from jax.experimental import pallas as pl
from jax.experimental.pallas import tpu as pltpu
from jax.sharding import Mesh
from jax.sharding import PartitionSpec as P

HI = lax.Precision.HIGHEST
EX_GROUP = 16
DP = ("yh", "x", "c")
XC = ("x", "c")
FS = ("yl", "z")


def mm(a, b, dims, prec=HI):
    return lax.dot_general(a, b, (dims, ((), ())), precision=prec, preferred_element_type=jnp.float32)

def factor_block(d_ref, w_ref):
    nb = 128
    full = (8, nb)
    xs = [d_ref[8 * v: 8 * v + 8, :] for v in range(nb // 8)]
    ws = [w_ref[8 * v: 8 * v + 8, :] for v in range(nb // 8)]
    for p in range(nb // 8):
        base = 8 * p
        xr = [jnp.broadcast_to(xs[p][i:i + 1, :], full) for i in range(8)]
        wr = [jnp.broadcast_to(ws[p][i:i + 1, :], full) for i in range(8)]
        s = [[jnp.broadcast_to(xr[i][:, base + j:base + j + 1], full) for j in range(i + 1)] for i in range(8)]
        m = [[None] * 8 for _ in range(8)]
        inv = [None] * 4
        for k in range(0, 8, 2):
            a, b, d = s[k][k], s[k + 1][k], s[k + 1][k + 1]
            det = 1.0 / (a * d - b * b)
            ia, ib, id_ = d * det, b * det, a * det
            inv[k // 2] = (ia, ib, id_)
            for i in range(k + 2, 8):
                m[i][k] = s[i][k] * ia - s[i][k + 1] * ib
                m[i][k + 1] = s[i][k + 1] * id_ - s[i][k] * ib
                for j in range(k + 2, i + 1):
                    s[i][j] = s[i][j] - (m[i][k] * s[j][k] + m[i][k + 1] * s[j][k + 1])
        for i in range(2, 8):
            for k in range(0, i - i % 2, 2):
                xr[i] = xr[i] - (m[i][k] * xr[k] + m[i][k + 1] * xr[k + 1])
                wr[i] = wr[i] - (m[i][k] * wr[k] + m[i][k + 1] * wr[k + 1])
        for k in range(0, 8, 2):
            a, b = s[k][k], s[k + 1][k]
            w_ref[base + k: base + k + 1, :] = (wr[k] * lax.rsqrt(a))[0:1, :]
            ratio = b / a
            low = (wr[k + 1] - ratio * wr[k]) * lax.rsqrt(s[k + 1][k + 1] - ratio * b)
            w_ref[base + k + 1: base + k + 2, :] = low[0:1, :]
        if p == nb // 8 - 1:
            break
        xv, wv = [None] * 8, [None] * 8
        for k in range(6, -1, -2):
            ia, ib, id_ = inv[k // 2]
            for rows, out in ((xr, xv), (wr, wv)):
                out[k] = rows[k] * ia - rows[k + 1] * ib
                out[k + 1] = rows[k + 1] * id_ - rows[k] * ib
                for i in range(k + 2, 8):
                    out[k] = out[k] - m[i][k] * out[i]
                    out[k + 1] = out[k + 1] - m[i][k + 1] * out[i]
        for q in range(p + 1, nb // 8):
            cols = [jnp.broadcast_to(xs[q][:, base + i:base + i + 1], full) for i in range(8)]
            for i in range(8):
                xs[q] = xs[q] - cols[i] * xv[i]
                ws[q] = ws[q] - cols[i] * wv[i]

def products_kernel(at_ref, tiles_ref, sketch_ref, gram_ref, sums_ref, features_ref):
    groups, half, lanes = tiles_ref.shape
    width = lanes // 2
    for g in range(groups):
        to = ((g % (groups // 2)) * 2 + g // (groups // 2)) * 2 * half
        tile = tiles_ref[g]
        features_ref[to:to + half, :] = tile[:, :width]
        features_ref[to + half:to + 2 * half, :] = tile[:, width:]
    rows = 4 * half
    features = features_ref[...]
    own = features_ref[pl.ds(pl.multiple_of(at_ref[0] * rows, rows), rows), :]
    inner = mm(own, features, ((1,), (1,)))
    scores = mm(own, sketch_ref[...], ((1,), (0,)))
    at = 0
    for part in (inner, scores, gram_ref[...]):
        for o in range(0, part.shape[1], lanes):
            sums_ref[at:at + part.shape[0], :] = part[:, o:o + lanes]
            at += part.shape[0]
    sums_ref[at:, :] = jnp.zeros((sums_ref.shape[0] - at, lanes), jnp.float32)


def products(block, tiles, sketch, gram_rows):
    vmem = pl.BlockSpec(memory_space=pltpu.VMEM)
    return pl.pallas_call(
        products_kernel,
        out_shape=(jax.ShapeDtypeStruct((512, 128), jnp.float32), jax.ShapeDtypeStruct((256, 64), jnp.float32)),
        in_specs=[pl.BlockSpec(memory_space=pltpu.SMEM), vmem, vmem, vmem],
        out_specs=(vmem, vmem),
        compiler_params=pltpu.CompilerParams(vmem_limit_bytes=24 * 1024 * 1024),
        name="products",
    )(block, tiles, sketch, gram_rows)


def finish_kernel(at_ref, sums_ref, sums2_ref, f_ref, s_ref, ns_ref, co_ref, a_ref, x_ref, k_ref, p_ref, d_ref, w_ref):
    n = a_ref.shape[0]
    own, e = f_ref.shape[1], f_ref.shape[0]
    across = sums_ref.shape[0]
    rows, cut = e // (2 * across), n // (2 * across)
    for side in range(2):
        core = at_ref[1] if side == 0 else 1 - at_ref[1]
        sums = sums_ref if side == 0 else sums2_ref
        for b in range(across):
            at = 0
            for to, height in ((k_ref, rows), (p_ref, rows), (a_ref, cut)):
                place = pl.ds(pl.multiple_of((2 * b + core) * height, height), height)
                for o in range(0, to.shape[1], 128):
                    to[place, o:o + 128] = sums[b, at:at + height, :]
                    at += height
    k = k_ref[...]
    p = p_ref[...]
    er = lax.broadcasted_iota(jnp.int32, (e, e), 0)
    ec = lax.broadcasted_iota(jnp.int32, (e, e), 1)
    total_sq = jnp.sum(jnp.sum(jnp.where(er == ec, k, 0.0), axis=0, keepdims=True), axis=1, keepdims=True)
    c = 16.0 / (total_sq + 1e-6)
    q = p + mm(k * c, p, ((1,), (0,)))
    x_ref[:own, :] = s_ref[...] + mm(f_ref[...] * c, p, ((0,), (0,)))
    x_ref[own:, :] = q
    pq = p + q
    pc = p * c
    for o in range(0, n, 128):
        a_ref[o:o + 128, o:] = a_ref[o:o + 128, o:] + mm(pc[:, o:o + 128], pq[:, o:], ((0,), (0,)))
    ri = lax.broadcasted_iota(jnp.int32, (128, 128), 0)
    ci = lax.broadcasted_iota(jnp.int32, (128, 128), 1)

    def step(b, carry):
        o = pl.multiple_of(b * 128, 128)
        d_ref[...] = a_ref[pl.ds(o, 128), pl.ds(o, 128)]
        w_ref[...] = jnp.where(ri == ci, 1.0, 0.0)
        factor_block(d_ref, w_ref)
        w = w_ref[...]
        x_ref[:, pl.ds(o, 128)] = mm(x_ref[:, pl.ds(o, 128)], w, ((1,), (1,)))
        for at in range(0, n - 128, 128):
            @pl.when(b * 128 == at)
            def _(at=at):
                r = mm(w, a_ref[at:at + 128, at + 128:], ((1,), (0,)))
                x_ref[:, at + 128:] = x_ref[:, at + 128:] - mm(x_ref[:, at:at + 128], r, ((1,), (0,)))
                for o in range(at + 128, n, 128):
                    a_ref[o:o + 128, o:] = a_ref[o:o + 128, o:] - mm(r[:, o - at - 128:o - at], r[:, o - at - 128:], ((0,), (0,)))
        return carry

    lax.fori_loop(0, n // 128, step, 0)
    ns_ref[...] = x_ref[:own, :]
    coefs = x_ref[own:, :]
    mean = jnp.sum(coefs * coefs, axis=0, keepdims=True) / e
    mine = x_ref[pl.ds(pl.multiple_of(own + at_ref[0] * EX_GROUP, EX_GROUP), EX_GROUP), :]
    co_ref[...] = mine / jnp.sqrt(mean + 1e-6)


def finish(at, sums, sums2, f, s):
    n, own, e = s.shape[1], s.shape[0], f.shape[0]
    vmem = pl.BlockSpec(memory_space=pltpu.VMEM)
    return pl.pallas_call(
        finish_kernel,
        out_shape=(jax.ShapeDtypeStruct((own, n), jnp.float32), jax.ShapeDtypeStruct((EX_GROUP, n), jnp.float32)),
        in_specs=[pl.BlockSpec(memory_space=pltpu.SMEM)] + [vmem] * 4,
        out_specs=(vmem, vmem),
        scratch_shapes=[
            pltpu.VMEM((n, n), jnp.float32),
            pltpu.VMEM((own + e, n), jnp.float32),
            pltpu.VMEM((e, e), jnp.float32),
            pltpu.VMEM((e, n), jnp.float32),
            pltpu.VMEM((128, 128), jnp.float32),
            pltpu.VMEM((128, 128), jnp.float32),
        ],
        compiler_params=pltpu.CompilerParams(vmem_limit_bytes=40 * 1024 * 1024),
        name="finish",
    )(at, sums, sums2, f, s)


def exchange(x, axes):
    return lax.all_to_all(x, axes, 0, 0, tiled=True)


def spread(x, axes):
    return exchange(jnp.broadcast_to(x[None], (lax.axis_size(axes),) + x.shape), axes)


def outer_kernel(part_ref, seg_ref, out_ref):
    both = jnp.sum(part_ref[...], axis=0)
    tokens, width = both.shape[0], both.shape[1] // 2
    half = EX_GROUP // 2
    left = both[:, :width]
    col = lax.broadcasted_iota(jnp.int32, (width, width * half), 1)
    row = lax.broadcasted_iota(jnp.int32, (width, width * half), 0)
    repeat = jnp.where(col // half == row, 1.0, 0.0)
    wide = mm(left, repeat, ((1,), (0,)))
    slot = lax.broadcasted_iota(jnp.int32, (tokens, width * half), 1) % half
    seg = seg_ref[...]
    low = jnp.where(slot == seg, wide, 0.0)
    high = jnp.where(slot + half == seg, wide, 0.0)
    lane = lax.broadcasted_iota(jnp.int32, both.shape, 1)
    right = jnp.concatenate([both[:, width:], both[:, width:]], axis=1)
    right_low = jnp.where(lane < width, right, 0.0)
    right_high = jnp.where(lane < width, 0.0, right)
    out = mm(low, right_low, ((0,), (0,))) + mm(high, right_high, ((0,), (0,)))
    out_ref[...] = out.reshape(out_ref.shape)


def outer(parts, seg):
    width = parts.shape[2] // 2
    return pl.pallas_call(
        outer_kernel,
        out_shape=jax.ShapeDtypeStruct((width, EX_GROUP // 2, 2 * width), jnp.float32),
        in_specs=[pl.BlockSpec(memory_space=pltpu.VMEM)] * 2,
        out_specs=pl.BlockSpec(memory_space=pltpu.VMEM),
        compiler_params=pltpu.CompilerParams(vmem_limit_bytes=24 * 1024 * 1024),
        name="outer",
    )(parts, seg)


def per_device(inputs, out_grads, proj_in, proj_out, segment_ids, sketch):
    owners = lax.axis_size(FS)
    blocks = lax.axis_size(XC)
    tokens = inputs.shape[0]
    width = proj_in.shape[1]
    rank = sketch.shape[1]
    half = EX_GROUP // 2
    own_tokens = tokens // owners
    place = lax.axis_index(FS)
    block = lax.axis_index(XC)

    cut = rank // blocks
    gram_rows = mm(lax.dynamic_slice_in_dim(sketch, block * cut, cut, 1), sketch, ((0,), (0,)))

    segments = segment_ids[0]
    onehot = segments[:, None] == jnp.arange(EX_GROUP, dtype=jnp.int32)[None, :]
    counts = jnp.sum(onehot.astype(jnp.float32), axis=0)
    count_tile = jnp.repeat(counts.reshape(2, half).T, width, axis=1)
    own_segments = lax.dynamic_slice_in_dim(segments, place * own_tokens, own_tokens, 0)[:, None]

    projected = jnp.concatenate(
        [
            jnp.dot(inputs, proj_in, preferred_element_type=jnp.float32),
            jnp.dot(out_grads, proj_out, preferred_element_type=jnp.float32),
        ],
        axis=1,
    )
    parts = exchange(projected.reshape(4, -1, 2 * width), "yl")
    parts = exchange(jnp.sum(parts, axis=0).reshape(-1, own_tokens, 2 * width), "z")
    partial_features = outer(parts, own_segments)
    tile = jnp.sum(exchange(partial_features, FS), axis=0) / count_tile
    tiles = spread(tile, DP)
    sums, features = products(block[None], tiles, sketch, gram_rows)
    chunk = jnp.sum(exchange(sums.reshape(owners, -1, 128), FS), axis=0)
    sums = spread(chunk, FS).reshape(sums.shape)[: 2 * EX_GROUP * 6 + cut * 4]
    sums = spread(sums, "x")
    other = lax.ppermute(sums, "c", [(0, 1), (1, 0)])
    at = jnp.stack([block * 2 + lax.axis_index("yh"), lax.axis_index("c")])
    return finish(at, sums, other, features, sketch)


def solution(mesh):
    fine = Mesh(mesh.devices.reshape(2, 4, 2, 4, 16), ("yh", "x", "c", "yl", "z"))
    return jax.shard_map(
        per_device,
        mesh=fine,
        in_specs=(P(DP, FS), P(DP, FS), P(FS, None), P(FS, None), P(DP, None), P(FS, None)),
        out_specs=(P(FS, None), P(DP, None)),
        check_vma=False,
    )
```

```python
import functools

import jax
import jax.numpy as jnp
from jax import lax
from jax.experimental import pallas as pl
from jax.experimental.pallas import tpu as pltpu
from jax.sharding import Mesh
from jax.sharding import PartitionSpec as P

HI = lax.Precision.HIGHEST
EX_GROUP = 16
DP = ("yh", "x", "c")
XC = ("x", "c")
FS = ("yl", "zh", "zl")
NEAR = ("yl", "zl")
FAR = ("zh",)


def mm(a, b, dims, prec=HI):
    return lax.dot_general(a, b, (dims, ((), ())), precision=prec, preferred_element_type=jnp.float32)

def factor_block(d_ref, w_ref):
    nb = 128
    full = (8, nb)
    xs = [d_ref[8 * v: 8 * v + 8, :] for v in range(nb // 8)]
    ws = [w_ref[8 * v: 8 * v + 8, :] for v in range(nb // 8)]
    for p in range(nb // 8):
        base = 8 * p
        xr = [jnp.broadcast_to(xs[p][i:i + 1, :], full) for i in range(8)]
        wr = [jnp.broadcast_to(ws[p][i:i + 1, :], full) for i in range(8)]
        s = [[jnp.broadcast_to(xr[i][:, base + j:base + j + 1], full) for j in range(i + 1)] for i in range(8)]
        m = [[None] * 8 for _ in range(8)]
        inv = [None] * 4
        for k in range(0, 8, 2):
            a, b, d = s[k][k], s[k + 1][k], s[k + 1][k + 1]
            det = 1.0 / (a * d - b * b)
            ia, ib, id_ = d * det, b * det, a * det
            inv[k // 2] = (ia, ib, id_)
            for i in range(k + 2, 8):
                m[i][k] = s[i][k] * ia - s[i][k + 1] * ib
                m[i][k + 1] = s[i][k + 1] * id_ - s[i][k] * ib
                for j in range(k + 2, i + 1):
                    s[i][j] = s[i][j] - (m[i][k] * s[j][k] + m[i][k + 1] * s[j][k + 1])
        for i in range(2, 8):
            for k in range(0, i - i % 2, 2):
                xr[i] = xr[i] - (m[i][k] * xr[k] + m[i][k + 1] * xr[k + 1])
                wr[i] = wr[i] - (m[i][k] * wr[k] + m[i][k + 1] * wr[k + 1])
        for k in range(0, 8, 2):
            a, b = s[k][k], s[k + 1][k]
            w_ref[base + k: base + k + 1, :] = (wr[k] * lax.rsqrt(a))[0:1, :]
            ratio = b / a
            low = (wr[k + 1] - ratio * wr[k]) * lax.rsqrt(s[k + 1][k + 1] - ratio * b)
            w_ref[base + k + 1: base + k + 2, :] = low[0:1, :]
        if p == nb // 8 - 1:
            break
        xv, wv = [None] * 8, [None] * 8
        for k in range(6, -1, -2):
            ia, ib, id_ = inv[k // 2]
            for rows, out in ((xr, xv), (wr, wv)):
                out[k] = rows[k] * ia - rows[k + 1] * ib
                out[k + 1] = rows[k + 1] * id_ - rows[k] * ib
                for i in range(k + 2, 8):
                    out[k] = out[k] - m[i][k] * out[i]
                    out[k + 1] = out[k + 1] - m[i][k + 1] * out[i]
        for q in range(p + 1, nb // 8):
            cols = [jnp.broadcast_to(xs[q][:, base + i:base + i + 1], full) for i in range(8)]
            for i in range(8):
                xs[q] = xs[q] - cols[i] * xv[i]
                ws[q] = ws[q] - cols[i] * wv[i]

def products_kernel(at_ref, tiles_ref, sketch_ref, gram_ref, sums_ref, features_ref):
    groups, half, lanes = tiles_ref.shape
    width = lanes // 2
    for g in range(groups):
        to = ((g % (groups // 2)) * 2 + g // (groups // 2)) * 2 * half
        tile = tiles_ref[g]
        features_ref[to:to + half, :] = tile[:, :width]
        features_ref[to + half:to + 2 * half, :] = tile[:, width:]
    rows = 4 * half
    features = features_ref[...]
    own = features_ref[pl.ds(pl.multiple_of(at_ref[0] * rows, rows), rows), :]
    inner = mm(own, features, ((1,), (1,)))
    scores = mm(own, sketch_ref[...], ((1,), (0,)))
    at = 0
    for part in (inner, scores, gram_ref[...]):
        for o in range(0, part.shape[1], lanes):
            sums_ref[at:at + part.shape[0], :] = part[:, o:o + lanes]
            at += part.shape[0]
    sums_ref[at:, :] = jnp.zeros((sums_ref.shape[0] - at, lanes), jnp.float32)


def products(block, tiles, sketch, gram_rows):
    vmem = pl.BlockSpec(memory_space=pltpu.VMEM)
    return pl.pallas_call(
        products_kernel,
        out_shape=(jax.ShapeDtypeStruct((384, 128), jnp.float32), jax.ShapeDtypeStruct((256, 64), jnp.float32)),
        in_specs=[pl.BlockSpec(memory_space=pltpu.SMEM), vmem, vmem, vmem],
        out_specs=(vmem, vmem),
        compiler_params=pltpu.CompilerParams(vmem_limit_bytes=24 * 1024 * 1024),
        name="products",
    )(block, tiles, sketch, gram_rows)


def finish_kernel(at_ref, sums_ref, sums2_ref, f_ref, s_ref, ns_ref, co_ref, a_ref, x_ref, k_ref, p_ref, g_ref, d_ref, w_ref):
    n = a_ref.shape[0]
    own, e = f_ref.shape[1], f_ref.shape[0]
    across = sums_ref.shape[0]
    rows, cut = e // (2 * across), g_ref.shape[0] // (2 * across)
    for side in range(2):
        core = at_ref[1] if side == 0 else 1 - at_ref[1]
        sums = sums_ref if side == 0 else sums2_ref
        for b in range(across):
            at = 0
            for to, height in ((k_ref, rows), (p_ref, rows), (g_ref, cut)):
                place = pl.ds(pl.multiple_of((2 * b + core) * height, height), height)
                for o in range(0, to.shape[1], 128):
                    to[place, o:o + 128] = sums[b, at:at + height, :]
                    at += height
    k = k_ref[...]
    p = p_ref[...]
    er = lax.broadcasted_iota(jnp.int32, (e, e), 0)
    ec = lax.broadcasted_iota(jnp.int32, (e, e), 1)
    total_sq = jnp.sum(jnp.sum(jnp.where(er == ec, k, 0.0), axis=0, keepdims=True), axis=1, keepdims=True)
    c = 16.0 / (total_sq + 1e-6)
    q = p + mm(k * c, p, ((1,), (0,)))
    x_ref[:own, :] = s_ref[...] + mm(f_ref[...] * c, p, ((0,), (0,)))
    x_ref[own:, :] = q
    pq = p + q
    pc = p * c
    at = 0
    for o in range(0, n, 128):
        update = mm(pc[:, o:o + 128], pq[:, o:], ((0,), (0,)))
        for to in range(o, n, 128):
            a_ref[o:o + 128, to:to + 128] = g_ref[at:at + 128, :] + update[:, to - o:to - o + 128]
            at += 128
    ri = lax.broadcasted_iota(jnp.int32, (128, 128), 0)
    ci = lax.broadcasted_iota(jnp.int32, (128, 128), 1)

    def step(b, carry):
        o = pl.multiple_of(b * 128, 128)
        d_ref[...] = a_ref[pl.ds(o, 128), pl.ds(o, 128)]
        w_ref[...] = jnp.where(ri == ci, 1.0, 0.0)
        factor_block(d_ref, w_ref)
        w = w_ref[...]
        x_ref[:, pl.ds(o, 128)] = mm(x_ref[:, pl.ds(o, 128)], w, ((1,), (1,)))
        for at in range(0, n - 128, 128):
            @pl.when(b * 128 == at)
            def _(at=at):
                r = mm(w, a_ref[at:at + 128, at + 128:], ((1,), (0,)))
                x_ref[:, at + 128:] = x_ref[:, at + 128:] - mm(x_ref[:, at:at + 128], r, ((1,), (0,)))
                for o in range(at + 128, n, 128):
                    a_ref[o:o + 128, o:] = a_ref[o:o + 128, o:] - mm(r[:, o - at - 128:o - at], r[:, o - at - 128:], ((0,), (0,)))
        return carry

    lax.fori_loop(0, n // 128, step, 0)
    ns_ref[...] = x_ref[:own, :]
    coefs = x_ref[own:, :]
    mean = jnp.sum(coefs * coefs, axis=0, keepdims=True) / e
    mine = x_ref[pl.ds(pl.multiple_of(own + at_ref[0] * EX_GROUP, EX_GROUP), EX_GROUP), :]
    co_ref[...] = mine / jnp.sqrt(mean + 1e-6)


def finish(at, sums, sums2, f, s):
    n, own, e = s.shape[1], s.shape[0], f.shape[0]
    vmem = pl.BlockSpec(memory_space=pltpu.VMEM)
    return pl.pallas_call(
        finish_kernel,
        out_shape=(jax.ShapeDtypeStruct((own, n), jnp.float32), jax.ShapeDtypeStruct((EX_GROUP, n), jnp.float32)),
        in_specs=[pl.BlockSpec(memory_space=pltpu.SMEM)] + [vmem] * 4,
        out_specs=(vmem, vmem),
        scratch_shapes=[
            pltpu.VMEM((n, n), jnp.float32),
            pltpu.VMEM((own + e, n), jnp.float32),
            pltpu.VMEM((e, e), jnp.float32),
            pltpu.VMEM((e, n), jnp.float32),
            pltpu.VMEM((n * (n + 128) // 256, 128), jnp.float32),
            pltpu.VMEM((128, 128), jnp.float32),
            pltpu.VMEM((128, 128), jnp.float32),
        ],
        compiler_params=pltpu.CompilerParams(vmem_limit_bytes=40 * 1024 * 1024),
        name="finish",
    )(at, sums, sums2, f, s)


def exchange(x, axes):
    return lax.all_to_all(x, axes, 0, 0, tiled=True)


def spread(x, axes):
    return exchange(jnp.broadcast_to(x[None], (lax.axis_size(axes),) + x.shape), axes)


def outer_kernel(part_ref, seg_ref, out_ref):
    both = jnp.sum(part_ref[...], axis=0)
    tokens, width = both.shape[0], both.shape[1] // 2
    half = EX_GROUP // 2
    left = both[:, :width]
    col = lax.broadcasted_iota(jnp.int32, (width, width * half), 1)
    row = lax.broadcasted_iota(jnp.int32, (width, width * half), 0)
    repeat = jnp.where(col // half == row, 1.0, 0.0)
    wide = mm(left, repeat, ((1,), (0,)))
    slot = lax.broadcasted_iota(jnp.int32, (tokens, width * half), 1) % half
    seg = seg_ref[...]
    low = jnp.where(slot == seg, wide, 0.0)
    high = jnp.where(slot + half == seg, wide, 0.0)
    lane = lax.broadcasted_iota(jnp.int32, both.shape, 1)
    right = jnp.concatenate([both[:, width:], both[:, width:]], axis=1)
    right_low = jnp.where(lane < width, right, 0.0)
    right_high = jnp.where(lane < width, 0.0, right)
    out = mm(low, right_low, ((0,), (0,))) + mm(high, right_high, ((0,), (0,)))
    out_ref[...] = out.reshape(out_ref.shape)


def outer(parts, seg):
    width = parts.shape[2] // 2
    return pl.pallas_call(
        outer_kernel,
        out_shape=jax.ShapeDtypeStruct((width, EX_GROUP // 2, 2 * width), jnp.float32),
        in_specs=[pl.BlockSpec(memory_space=pltpu.VMEM)] * 2,
        out_specs=pl.BlockSpec(memory_space=pltpu.VMEM),
        compiler_params=pltpu.CompilerParams(vmem_limit_bytes=24 * 1024 * 1024),
        name="outer",
    )(parts, seg)


def per_device(inputs, out_grads, proj_in, proj_out, segment_ids, sketch):
    owners = lax.axis_size(FS)
    blocks = lax.axis_size(XC)
    tokens = inputs.shape[0]
    width = proj_in.shape[1]
    rank = sketch.shape[1]
    half = EX_GROUP // 2
    own_tokens = tokens // owners
    place = lax.axis_index(NEAR + FAR)
    block = lax.axis_index(XC)

    gram = mm(sketch, sketch, ((0,), (0,)))
    upper = [gram[o:o + 128, to:to + 128] for o in range(0, rank, 128) for to in range(o, rank, 128)]
    cut = len(upper) * 128 // blocks
    gram_rows = lax.dynamic_slice_in_dim(jnp.concatenate(upper, axis=0), block * cut, cut, 0)

    segments = segment_ids[0]
    onehot = segments[:, None] == jnp.arange(EX_GROUP, dtype=jnp.int32)[None, :]
    counts = jnp.sum(onehot.astype(jnp.float32), axis=0)
    count_tile = jnp.repeat(counts.reshape(2, half).T, width, axis=1)
    own_segments = lax.dynamic_slice_in_dim(segments, place * own_tokens, own_tokens, 0)[:, None]

    projected = jnp.concatenate(
        [
            jnp.dot(inputs, proj_in, preferred_element_type=jnp.float32),
            jnp.dot(out_grads, proj_out, preferred_element_type=jnp.float32),
        ],
        axis=1,
    )
    parts = exchange(projected.reshape(lax.axis_size(NEAR), -1, 2 * width), NEAR)
    parts = exchange(jnp.sum(parts, axis=0).reshape(-1, own_tokens, 2 * width), FAR)
    partial_features = outer(parts, own_segments)
    tile = jnp.sum(exchange(partial_features, FS), axis=0) / count_tile
    tiles = spread(tile, DP)
    sums, features = products(block[None], tiles, sketch, gram_rows)
    chunk = jnp.sum(exchange(sums.reshape(owners, 1, -1), FS), axis=0)
    sums = spread(chunk, FS).reshape(sums.shape)[: 2 * EX_GROUP * 6 + cut]
    sums = spread(sums, "x")
    other = lax.ppermute(sums, "c", [(0, 1), (1, 0)])
    at = jnp.stack([block * 2 + lax.axis_index("yh"), lax.axis_index("c")])
    return finish(at, sums, other, features, sketch)


def solution(mesh):
    fine = Mesh(mesh.devices.reshape(2, 4, 2, 4, 4, 4), ("yh", "x", "c", "yl", "zh", "zl"))
    return jax.shard_map(
        per_device,
        mesh=fine,
        in_specs=(P(DP, FS), P(DP, FS), P(FS, None), P(FS, None), P(DP, None), P(FS, None)),
        out_specs=(P(FS, None), P(DP, None)),
        check_vma=False,
    )
```

```python
import functools

import jax
import jax.numpy as jnp
from jax import lax
from jax.experimental import pallas as pl
from jax.experimental.pallas import tpu as pltpu
from jax.sharding import Mesh
from jax.sharding import PartitionSpec as P

HI = lax.Precision.HIGHEST
EX_GROUP = 16
DP = ("yh", "x", "c")
XC = ("x", "c")
FS = ("yl", "zh", "zl")
NEAR = ("yl", "zl")
FAR = ("zh",)


def mm(a, b, dims, prec=HI):
    return lax.dot_general(a, b, (dims, ((), ())), precision=prec, preferred_element_type=jnp.float32)

def factor_block(d_ref, w_ref):
    nb = 128
    full = (8, nb)
    xs = [d_ref[8 * v: 8 * v + 8, :] for v in range(nb // 8)]
    ws = [w_ref[8 * v: 8 * v + 8, :] for v in range(nb // 8)]
    for p in range(nb // 8):
        base = 8 * p
        xr = [jnp.broadcast_to(xs[p][i:i + 1, :], full) for i in range(8)]
        wr = [jnp.broadcast_to(ws[p][i:i + 1, :], full) for i in range(8)]
        s = [[jnp.broadcast_to(xr[i][:, base + j:base + j + 1], full) for j in range(i + 1)] for i in range(8)]
        m = [[None] * 8 for _ in range(8)]
        inv = [None] * 4
        for k in range(0, 8, 2):
            a, b, d = s[k][k], s[k + 1][k], s[k + 1][k + 1]
            det = 1.0 / (a * d - b * b)
            ia, ib, id_ = d * det, b * det, a * det
            inv[k // 2] = (ia, ib, id_)
            for i in range(k + 2, 8):
                m[i][k] = s[i][k] * ia - s[i][k + 1] * ib
                m[i][k + 1] = s[i][k + 1] * id_ - s[i][k] * ib
                for j in range(k + 2, i + 1):
                    s[i][j] = s[i][j] - (m[i][k] * s[j][k] + m[i][k + 1] * s[j][k + 1])
        for i in range(2, 8):
            for k in range(0, i - i % 2, 2):
                xr[i] = xr[i] - (m[i][k] * xr[k] + m[i][k + 1] * xr[k + 1])
                wr[i] = wr[i] - (m[i][k] * wr[k] + m[i][k + 1] * wr[k + 1])
        for k in range(0, 8, 2):
            a, b = s[k][k], s[k + 1][k]
            w_ref[base + k: base + k + 1, :] = (wr[k] * lax.rsqrt(a))[0:1, :]
            ratio = b / a
            low = (wr[k + 1] - ratio * wr[k]) * lax.rsqrt(s[k + 1][k + 1] - ratio * b)
            w_ref[base + k + 1: base + k + 2, :] = low[0:1, :]
        if p == nb // 8 - 1:
            break
        xv, wv = [None] * 8, [None] * 8
        for k in range(6, -1, -2):
            ia, ib, id_ = inv[k // 2]
            for rows, out in ((xr, xv), (wr, wv)):
                out[k] = rows[k] * ia - rows[k + 1] * ib
                out[k + 1] = rows[k + 1] * id_ - rows[k] * ib
                for i in range(k + 2, 8):
                    out[k] = out[k] - m[i][k] * out[i]
                    out[k + 1] = out[k + 1] - m[i][k + 1] * out[i]
        for q in range(p + 1, nb // 8):
            cols = [jnp.broadcast_to(xs[q][:, base + i:base + i + 1], full) for i in range(8)]
            for i in range(8):
                xs[q] = xs[q] - cols[i] * xv[i]
                ws[q] = ws[q] - cols[i] * wv[i]

def products_kernel(at_ref, tiles_ref, sketch_ref, gram_ref, sums_ref, features_ref):
    groups, half, lanes = tiles_ref.shape
    width = lanes // 2
    for g in range(groups):
        to = ((g % (groups // 2)) * 2 + g // (groups // 2)) * 2 * half
        tile = tiles_ref[g]
        features_ref[to:to + half, :] = tile[:, :width]
        features_ref[to + half:to + 2 * half, :] = tile[:, width:]
    rows = 4 * half
    features = features_ref[...]
    own = features_ref[pl.ds(pl.multiple_of(at_ref[0] * rows, rows), rows), :]
    inner = mm(own, features, ((1,), (1,)))
    scores = mm(own, sketch_ref[...], ((1,), (0,)))
    at = 0
    for part in (inner, scores, gram_ref[...]):
        for o in range(0, part.shape[1], lanes):
            sums_ref[at:at + part.shape[0], :] = part[:, o:o + lanes]
            at += part.shape[0]
    sums_ref[at:, :] = jnp.zeros((sums_ref.shape[0] - at, lanes), jnp.float32)


def products(block, tiles, sketch, gram_rows):
    vmem = pl.BlockSpec(memory_space=pltpu.VMEM)
    return pl.pallas_call(
        products_kernel,
        out_shape=(jax.ShapeDtypeStruct((384, 128), jnp.float32), jax.ShapeDtypeStruct((256, 64), jnp.float32)),
        in_specs=[pl.BlockSpec(memory_space=pltpu.SMEM), vmem, vmem, vmem],
        out_specs=(vmem, vmem),
        compiler_params=pltpu.CompilerParams(vmem_limit_bytes=24 * 1024 * 1024),
        name="products",
    )(block, tiles, sketch, gram_rows)


def finish_kernel(at_ref, sums_ref, sums2_ref, f_ref, s_ref, ns_ref, co_ref, a_ref, x_ref, k_ref, p_ref, g_ref, d_ref, w_ref):
    n = a_ref.shape[0]
    own, e = f_ref.shape[1], f_ref.shape[0]
    across = sums_ref.shape[0]
    rows, cut = e // (2 * across), g_ref.shape[0] // (2 * across)
    for side in range(2):
        core = at_ref[1] if side == 0 else 1 - at_ref[1]
        sums = sums_ref if side == 0 else sums2_ref
        for b in range(across):
            at = 0
            for to, height in ((k_ref, rows), (p_ref, rows), (g_ref, cut)):
                place = pl.ds(pl.multiple_of((2 * b + core) * height, height), height)
                for o in range(0, to.shape[1], 128):
                    to[place, o:o + 128] = sums[b, at:at + height, :]
                    at += height
    k = k_ref[...]
    p = p_ref[...]
    er = lax.broadcasted_iota(jnp.int32, (e, e), 0)
    ec = lax.broadcasted_iota(jnp.int32, (e, e), 1)
    total_sq = jnp.sum(jnp.sum(jnp.where(er == ec, k, 0.0), axis=0, keepdims=True), axis=1, keepdims=True)
    c = 16.0 / (total_sq + 1e-6)
    q = p + mm(k * c, p, ((1,), (0,)))
    x_ref[:own, :] = s_ref[...] + mm(f_ref[...] * c, p, ((0,), (0,)))
    x_ref[own:, :] = q
    pq = p + q
    pc = p * c
    at = 0
    for o in range(0, n, 128):
        update = mm(pc[:, o:o + 128], pq[:, o:], ((0,), (0,)))
        for to in range(o, n, 128):
            a_ref[o:o + 128, to:to + 128] = g_ref[at:at + 128, :] + update[:, to - o:to - o + 128]
            at += 128
    ri = lax.broadcasted_iota(jnp.int32, (128, 128), 0)
    ci = lax.broadcasted_iota(jnp.int32, (128, 128), 1)

    def step(b, carry):
        o = pl.multiple_of(b * 128, 128)
        d_ref[...] = a_ref[pl.ds(o, 128), pl.ds(o, 128)]
        w_ref[...] = jnp.where(ri == ci, 1.0, 0.0)
        factor_block(d_ref, w_ref)
        w = w_ref[...]
        x_ref[:, pl.ds(o, 128)] = mm(x_ref[:, pl.ds(o, 128)], w, ((1,), (1,)))
        for at in range(0, n - 128, 128):
            @pl.when(b * 128 == at)
            def _(at=at):
                r = mm(w, a_ref[at:at + 128, at + 128:], ((1,), (0,)))
                x_ref[:, at + 128:] = x_ref[:, at + 128:] - mm(x_ref[:, at:at + 128], r, ((1,), (0,)))
                for o in range(at + 128, n, 128):
                    a_ref[o:o + 128, o:] = a_ref[o:o + 128, o:] - mm(r[:, o - at - 128:o - at], r[:, o - at - 128:], ((0,), (0,)))
        return carry

    lax.fori_loop(0, n // 128, step, 0)
    ns_ref[...] = x_ref[:own, :]
    coefs = x_ref[own:, :]
    mean = jnp.sum(coefs * coefs, axis=0, keepdims=True) / e
    mine = x_ref[pl.ds(pl.multiple_of(own + at_ref[0] * EX_GROUP, EX_GROUP), EX_GROUP), :]
    co_ref[...] = mine / jnp.sqrt(mean + 1e-6)


def finish(at, sums, sums2, f, s):
    n, own, e = s.shape[1], s.shape[0], f.shape[0]
    vmem = pl.BlockSpec(memory_space=pltpu.VMEM)
    return pl.pallas_call(
        finish_kernel,
        out_shape=(jax.ShapeDtypeStruct((own, n), jnp.float32), jax.ShapeDtypeStruct((EX_GROUP, n), jnp.float32)),
        in_specs=[pl.BlockSpec(memory_space=pltpu.SMEM)] + [vmem] * 4,
        out_specs=(vmem, vmem),
        scratch_shapes=[
            pltpu.VMEM((n, n), jnp.float32),
            pltpu.VMEM((own + e, n), jnp.float32),
            pltpu.VMEM((e, e), jnp.float32),
            pltpu.VMEM((e, n), jnp.float32),
            pltpu.VMEM((n * (n + 128) // 256, 128), jnp.float32),
            pltpu.VMEM((128, 128), jnp.float32),
            pltpu.VMEM((128, 128), jnp.float32),
        ],
        compiler_params=pltpu.CompilerParams(vmem_limit_bytes=40 * 1024 * 1024),
        name="finish",
    )(at, sums, sums2, f, s)


def exchange(x, axes):
    return lax.all_to_all(x, axes, 0, 0, tiled=True)


def spread(x, axes):
    return exchange(jnp.broadcast_to(x[None], (lax.axis_size(axes),) + x.shape), axes)


def project_kernel(x_ref, y_ref, px_ref, py_ref, out_ref):
    left = lax.dot_general(px_ref[...], x_ref[...], (((1,), (1,)), ((), ())), preferred_element_type=jnp.float32)
    right = lax.dot_general(py_ref[...], y_ref[...], (((1,), (0,)), ((), ())), preferred_element_type=jnp.float32)
    width = left.shape[0]
    for c in range(out_ref.shape[0]):
        out_ref[c, :width, :] = left[:, c * 128:(c + 1) * 128]
        out_ref[c, width:, :] = right[:, c * 128:(c + 1) * 128]


def project(x, y, px, py):
    tokens, width = x.shape[0], px.shape[1]
    step = tokens // 4
    return pl.pallas_call(
        project_kernel,
        grid=(4,),
        out_shape=jax.ShapeDtypeStruct((tokens // 128, 2 * width, 128), jnp.float32),
        in_specs=[
            pl.BlockSpec((step, x.shape[1]), lambda i: (i, 0)),
            pl.BlockSpec((y.shape[1], step), lambda i: (0, i)),
            pl.BlockSpec((width, x.shape[1]), lambda i: (0, 0)),
            pl.BlockSpec((width, y.shape[1]), lambda i: (0, 0)),
        ],
        out_specs=pl.BlockSpec((step // 128, 2 * width, 128), lambda i: (i, 0, 0)),
        compiler_params=pltpu.CompilerParams(vmem_limit_bytes=16 * 1024 * 1024),
        name="project",
    )(x, y.T, px.T, py.T)


def fold_kernel(parts_ref, out_ref):
    out_ref[...] = jnp.sum(parts_ref[...], axis=0).T


def fold(parts):
    vmem = pl.BlockSpec(memory_space=pltpu.VMEM)
    return pl.pallas_call(
        fold_kernel,
        out_shape=jax.ShapeDtypeStruct((parts.shape[2], parts.shape[1]), jnp.float32),
        in_specs=[vmem],
        out_specs=vmem,
        compiler_params=pltpu.CompilerParams(vmem_limit_bytes=16 * 1024 * 1024),
        name="fold",
    )(parts)


def outer_kernel(part_ref, seg_ref, out_ref):
    both = jnp.sum(part_ref[...], axis=0)
    tokens, width = both.shape[0], both.shape[1] // 2
    half = EX_GROUP // 2
    left = both[:, :width]
    col = lax.broadcasted_iota(jnp.int32, (width, width * half), 1)
    row = lax.broadcasted_iota(jnp.int32, (width, width * half), 0)
    repeat = jnp.where(col // half == row, 1.0, 0.0)
    wide = mm(left, repeat, ((1,), (0,)))
    slot = lax.broadcasted_iota(jnp.int32, (tokens, width * half), 1) % half
    seg = seg_ref[...]
    low = jnp.where(slot == seg, wide, 0.0)
    high = jnp.where(slot + half == seg, wide, 0.0)
    lane = lax.broadcasted_iota(jnp.int32, both.shape, 1)
    right = jnp.concatenate([both[:, width:], both[:, width:]], axis=1)
    right_low = jnp.where(lane < width, right, 0.0)
    right_high = jnp.where(lane < width, 0.0, right)
    out = mm(low, right_low, ((0,), (0,))) + mm(high, right_high, ((0,), (0,)))
    out_ref[...] = out.reshape(out_ref.shape)


def outer(parts, seg):
    width = parts.shape[2] // 2
    return pl.pallas_call(
        outer_kernel,
        out_shape=jax.ShapeDtypeStruct((width, EX_GROUP // 2, 2 * width), jnp.float32),
        in_specs=[pl.BlockSpec(memory_space=pltpu.VMEM)] * 2,
        out_specs=pl.BlockSpec(memory_space=pltpu.VMEM),
        compiler_params=pltpu.CompilerParams(vmem_limit_bytes=24 * 1024 * 1024),
        name="outer",
    )(parts, seg)


def per_device(inputs, out_grads, proj_in, proj_out, segment_ids, sketch):
    owners = lax.axis_size(FS)
    blocks = lax.axis_size(XC)
    tokens = inputs.shape[0]
    width = proj_in.shape[1]
    rank = sketch.shape[1]
    half = EX_GROUP // 2
    own_tokens = tokens // owners
    place = lax.axis_index(NEAR + FAR)
    block = lax.axis_index(XC)

    gram = mm(sketch, sketch, ((0,), (0,)))
    upper = [gram[o:o + 128, to:to + 128] for o in range(0, rank, 128) for to in range(o, rank, 128)]
    cut = len(upper) * 128 // blocks
    gram_rows = lax.dynamic_slice_in_dim(jnp.concatenate(upper, axis=0), block * cut, cut, 0)

    segments = segment_ids[0]
    onehot = segments[:, None] == jnp.arange(EX_GROUP, dtype=jnp.int32)[None, :]
    counts = jnp.sum(onehot.astype(jnp.float32), axis=0)
    count_tile = jnp.repeat(counts.reshape(2, half).T, width, axis=1)
    own_segments = lax.dynamic_slice_in_dim(segments, place * own_tokens, own_tokens, 0)[:, None]

    parts = fold(exchange(project(inputs, out_grads, proj_in, proj_out), NEAR))
    parts = exchange(parts.reshape(-1, own_tokens, 2 * width), FAR)
    partial_features = outer(parts, own_segments)
    tile = jnp.sum(exchange(partial_features, FS), axis=0) / count_tile
    tiles = spread(tile, DP)
    sums, features = products(block[None], tiles, sketch, gram_rows)
    chunk = jnp.sum(exchange(sums.reshape(lax.axis_size(NEAR), -1, 128), NEAR), axis=0)
    chunk = jnp.sum(spread(chunk, FAR), axis=0)
    sums = spread(chunk, NEAR).reshape(sums.shape)[: 2 * EX_GROUP * 6 + cut]
    sums = spread(sums, "x")
    other = lax.ppermute(sums, "c", [(0, 1), (1, 0)])
    at = jnp.stack([block * 2 + lax.axis_index("yh"), lax.axis_index("c")])
    return finish(at, sums, other, features, sketch)


def solution(mesh):
    fine = Mesh(mesh.devices.reshape(2, 4, 2, 4, 4, 4), ("yh", "x", "c", "yl", "zh", "zl"))
    return jax.shard_map(
        per_device,
        mesh=fine,
        in_specs=(P(DP, FS), P(DP, FS), P(FS, None), P(FS, None), P(DP, None), P(FS, None)),
        out_specs=(P(FS, None), P(DP, None)),
        check_vma=False,
    )
```

```python
import functools

import jax
import jax.numpy as jnp
from jax import lax
from jax.experimental import pallas as pl
from jax.experimental.pallas import tpu as pltpu
from jax.sharding import Mesh
from jax.sharding import PartitionSpec as P

HI = lax.Precision.HIGHEST
EX_GROUP = 16
DP = ("yh", "x", "c")
XC = ("x", "c")
FS = ("yl", "zh", "zl")
NEAR = ("yl", "zl")
FAR = ("zh",)


def mm(a, b, dims, prec=HI):
    return lax.dot_general(a, b, (dims, ((), ())), precision=prec, preferred_element_type=jnp.float32)

def factor_block(d_ref, w_ref):
    nb = 128
    full = (8, nb)
    lane = lax.broadcasted_iota(jnp.int32, full, 1)
    xs = [d_ref[8 * v: 8 * v + 8, :] for v in range(nb // 8)]
    diag = [jnp.broadcast_to(xs[0][:, j:j + 1], full) for j in range(8)]
    for p in range(nb // 8):
        base = 8 * p
        here = (lane >= base) & (lane < base + 8)
        xr = [jnp.broadcast_to(xs[p][i:i + 1, :], full) for i in range(8)]
        s = [[jnp.broadcast_to(diag[j][i:i + 1, :], full) for j in range(i + 1)] for i in range(8)]
        xr = [jnp.where(here, jnp.where(lane == base + i, 1.0, 0.0), xr[i]) for i in range(8)]
        m = [[None] * 8 for _ in range(8)]
        inv = [None] * 4
        for k in range(0, 8, 2):
            a, b, d = s[k][k], s[k + 1][k], s[k + 1][k + 1]
            det = 1.0 / (a * d - b * b)
            ia, ib, id_ = d * det, b * det, a * det
            inv[k // 2] = (ia, ib, id_)
            for i in range(k + 2, 8):
                m[i][k] = s[i][k] * ia - s[i][k + 1] * ib
                m[i][k + 1] = s[i][k + 1] * id_ - s[i][k] * ib
                for j in range(k + 2, i + 1):
                    s[i][j] = s[i][j] - (m[i][k] * s[j][k] + m[i][k + 1] * s[j][k + 1])
        for i in range(2, 8):
            for k in range(0, i - i % 2, 2):
                xr[i] = xr[i] - (m[i][k] * xr[k] + m[i][k + 1] * xr[k + 1])
        for k in range(0, 8, 2):
            a, b = s[k][k], s[k + 1][k]
            ratio = b / a
            top = xr[k] * lax.rsqrt(a)
            low = (xr[k + 1] - ratio * xr[k]) * lax.rsqrt(s[k + 1][k + 1] - ratio * b)
            w_ref[base + k: base + k + 1, :] = jnp.where(lane < base + 8, top, 0.0)[0:1, :]
            w_ref[base + k + 1: base + k + 2, :] = jnp.where(lane < base + 8, low, 0.0)[0:1, :]
        if p == nb // 8 - 1:
            break
        q = p + 1
        f = [jnp.broadcast_to(xs[q][:, base + i:base + i + 1], full) for i in range(8)]
        diag = [jnp.broadcast_to(xs[q][:, base + 8 + j:base + 9 + j], full) for j in range(8)]
        z = [None] * 8
        for k in range(0, 8, 2):
            ia, ib, id_ = inv[k // 2]
            z[k] = f[k] * ia - f[k + 1] * ib
            z[k + 1] = f[k + 1] * id_ - f[k] * ib
            for i in range(k + 2, 8):
                f[i] = f[i] - (m[i][k] * f[k] + m[i][k + 1] * f[k + 1])
            for j in range(8):
                diag[j] = diag[j] - (
                    z[k] * jnp.broadcast_to(f[k][j:j + 1, :], full)
                    + z[k + 1] * jnp.broadcast_to(f[k + 1][j:j + 1, :], full)
                )
        rest = jnp.where(here, 0.0, xs[q])
        for k in range(0, 8, 2):
            rest = rest - (z[k] * xr[k] + z[k + 1] * xr[k + 1])
        xs[q] = rest
        xv = [None] * 8
        for k in range(6, -1, -2):
            ia, ib, id_ = inv[k // 2]
            xv[k] = xr[k] * ia - xr[k + 1] * ib
            xv[k + 1] = xr[k + 1] * id_ - xr[k] * ib
            for i in range(k + 2, 8):
                xv[k] = xv[k] - m[i][k] * xv[i]
                xv[k + 1] = xv[k + 1] - m[i][k + 1] * xv[i]
        for q in range(p + 2, nb // 8):
            cols = [jnp.broadcast_to(xs[q][:, base + i:base + i + 1], full) for i in range(8)]
            rest = jnp.where(here, 0.0, xs[q])
            xs[q] = rest - (
                ((cols[0] * xv[0] + cols[1] * xv[1]) + (cols[2] * xv[2] + cols[3] * xv[3]))
                + ((cols[4] * xv[4] + cols[5] * xv[5]) + (cols[6] * xv[6] + cols[7] * xv[7]))
            )


def products_kernel(at_ref, tiles_ref, sketch_ref, gram_ref, sums_ref, features_ref):
    groups, half, lanes = tiles_ref.shape
    width = lanes // 2
    for g in range(groups):
        to = ((g % (groups // 2)) * 2 + g // (groups // 2)) * 2 * half
        tile = tiles_ref[g]
        features_ref[to:to + half, :] = tile[:, :width]
        features_ref[to + half:to + 2 * half, :] = tile[:, width:]
    rows = 4 * half
    features = features_ref[...]
    own = features_ref[pl.ds(pl.multiple_of(at_ref[0] * rows, rows), rows), :]
    inner = mm(own, features, ((1,), (1,)))
    scores = mm(own, sketch_ref[...], ((1,), (0,)))
    at = 0
    for part in (inner, scores, gram_ref[...]):
        for o in range(0, part.shape[1], lanes):
            sums_ref[at:at + part.shape[0], :] = part[:, o:o + lanes]
            at += part.shape[0]
    sums_ref[at:, :] = jnp.zeros((sums_ref.shape[0] - at, lanes), jnp.float32)


def products(block, tiles, sketch, gram_rows):
    vmem = pl.BlockSpec(memory_space=pltpu.VMEM)
    return pl.pallas_call(
        products_kernel,
        out_shape=(jax.ShapeDtypeStruct((384, 128), jnp.float32), jax.ShapeDtypeStruct((256, 64), jnp.float32)),
        in_specs=[pl.BlockSpec(memory_space=pltpu.SMEM), vmem, vmem, vmem],
        out_specs=(vmem, vmem),
        compiler_params=pltpu.CompilerParams(vmem_limit_bytes=24 * 1024 * 1024),
        name="products",
    )(block, tiles, sketch, gram_rows)


def finish_kernel(at_ref, sums_ref, sums2_ref, f_ref, s_ref, ns_ref, co_ref, a_ref, x_ref, k_ref, p_ref, g_ref, d_ref, w_ref, wp_ref):
    n = a_ref.shape[0]
    own, e = f_ref.shape[1], f_ref.shape[0]
    across = sums_ref.shape[0]
    rows, cut = e // (2 * across), g_ref.shape[0] // (2 * across)
    for side in range(2):
        core = at_ref[1] if side == 0 else 1 - at_ref[1]
        sums = sums_ref if side == 0 else sums2_ref
        for b in range(across):
            at = 0
            for to, height in ((k_ref, rows), (p_ref, rows), (g_ref, cut)):
                place = pl.ds(pl.multiple_of((2 * b + core) * height, height), height)
                for o in range(0, to.shape[1], 128):
                    to[place, o:o + 128] = sums[b, at:at + height, :]
                    at += height
    k = k_ref[...]
    p = p_ref[...]
    er = lax.broadcasted_iota(jnp.int32, (e, e), 0)
    ec = lax.broadcasted_iota(jnp.int32, (e, e), 1)
    total_sq = jnp.sum(jnp.sum(jnp.where(er == ec, k, 0.0), axis=0, keepdims=True), axis=1, keepdims=True)
    c = 16.0 / (total_sq + 1e-6)
    q = p + mm(k * c, p, ((1,), (0,)))
    pq = p + q
    pc = p * c
    colid = lax.broadcasted_iota(jnp.int32, (128, n), 1)

    def next_block(o, t):
        w = w_ref[...]
        wp_ref[...] = w
        r = mm(w, a_ref[pl.ds(o, 128), pl.ds(t, 128)], ((1,), (0,)))
        d_ref[...] = a_ref[pl.ds(t, 128), pl.ds(t, 128)] - mm(r, r, ((0,), (0,)))

    d_ref[...] = g_ref[:128, :] + mm(pc[:, :128], pq[:, :128], ((0,), (0,)))
    x_ref[:own, :] = s_ref[...] + mm(f_ref[...] * c, p, ((0,), (0,)))
    x_ref[own:, :] = q
    at = 0
    for o in range(0, n, 128):
        update = mm(pc[:, o:o + 128], pq[:, o:], ((0,), (0,)))
        if o > 0:
            a_ref[o:o + 128, :o] = jnp.zeros((128, o), jnp.float32)
        for to in range(o, n, 128):
            a_ref[o:o + 128, to:to + 128] = g_ref[at:at + 128, :] + update[:, to - o:to - o + 128]
            at += 128
    factor_block(d_ref, w_ref)
    next_block(0, 128)

    def step(b, carry):
        o = pl.multiple_of(b * 128, 128)
        before = pl.multiple_of(o - 128, 128)
        wp = wp_ref[...]
        r = jnp.where(colid >= o, mm(wp, a_ref[pl.ds(before, 128), :], ((1,), (0,))), 0.0)
        y = mm(x_ref[:, pl.ds(before, 128)], wp, ((1,), (1,)))
        x_ref[:, pl.ds(before, 128)] = y
        x_ref[...] = x_ref[...] - mm(y, r, ((1,), (0,)))
        a_ref[...] = a_ref[...] - mm(r, r, ((0,), (0,)))
        factor_block(d_ref, w_ref)
        next_block(o, pl.multiple_of(jnp.minimum(o + 128, n - 128), 128))
        return carry

    lax.fori_loop(1, n // 128, step, 0)
    x_ref[:, n - 128:] = mm(x_ref[:, n - 128:], wp_ref[...], ((1,), (1,)))
    ns_ref[...] = x_ref[:own, :]
    coefs = x_ref[own:, :]
    mean = jnp.sum(coefs * coefs, axis=0, keepdims=True) / e
    mine = x_ref[pl.ds(pl.multiple_of(own + at_ref[0] * EX_GROUP, EX_GROUP), EX_GROUP), :]
    co_ref[...] = mine / jnp.sqrt(mean + 1e-6)


def finish(at, sums, sums2, f, s):
    n, own, e = s.shape[1], s.shape[0], f.shape[0]
    vmem = pl.BlockSpec(memory_space=pltpu.VMEM)
    return pl.pallas_call(
        finish_kernel,
        out_shape=(jax.ShapeDtypeStruct((own, n), jnp.float32), jax.ShapeDtypeStruct((EX_GROUP, n), jnp.float32)),
        in_specs=[pl.BlockSpec(memory_space=pltpu.SMEM)] + [vmem] * 4,
        out_specs=(vmem, vmem),
        scratch_shapes=[
            pltpu.VMEM((n, n), jnp.float32),
            pltpu.VMEM((own + e, n), jnp.float32),
            pltpu.VMEM((e, e), jnp.float32),
            pltpu.VMEM((e, n), jnp.float32),
            pltpu.VMEM((n * (n + 128) // 256, 128), jnp.float32),
            pltpu.VMEM((128, 128), jnp.float32),
            pltpu.VMEM((128, 128), jnp.float32),
            pltpu.VMEM((128, 128), jnp.float32),
        ],
        compiler_params=pltpu.CompilerParams(vmem_limit_bytes=40 * 1024 * 1024),
        name="finish",
    )(at, sums, sums2, f, s)


def exchange(x, axes):
    return lax.all_to_all(x, axes, 0, 0, tiled=True)


def spread(x, axes):
    return exchange(jnp.broadcast_to(x[None], (lax.axis_size(axes),) + x.shape), axes)


def project_kernel(x_ref, y_ref, px_ref, py_ref, out_ref):
    left = lax.dot_general(px_ref[...], x_ref[...], (((1,), (1,)), ((), ())), preferred_element_type=jnp.float32)
    right = lax.dot_general(py_ref[...], y_ref[...], (((1,), (0,)), ((), ())), preferred_element_type=jnp.float32)
    width = left.shape[0]
    for c in range(out_ref.shape[0]):
        out_ref[c, :width, :] = left[:, c * 128:(c + 1) * 128]
        out_ref[c, width:, :] = right[:, c * 128:(c + 1) * 128]


def project(x, y, px, py):
    tokens, width = x.shape[0], px.shape[1]
    step = tokens // 4
    return pl.pallas_call(
        project_kernel,
        grid=(4,),
        out_shape=jax.ShapeDtypeStruct((tokens // 128, 2 * width, 128), jnp.float32),
        in_specs=[
            pl.BlockSpec((step, x.shape[1]), lambda i: (i, 0)),
            pl.BlockSpec((y.shape[1], step), lambda i: (0, i)),
            pl.BlockSpec((width, x.shape[1]), lambda i: (0, 0)),
            pl.BlockSpec((width, y.shape[1]), lambda i: (0, 0)),
        ],
        out_specs=pl.BlockSpec((step // 128, 2 * width, 128), lambda i: (i, 0, 0)),
        name="project",
    )(x, y.T, px.T, py.T)


def fold_kernel(parts_ref, out_ref):
    out_ref[...] = jnp.sum(parts_ref[...], axis=0).T


def fold(parts):
    vmem = pl.BlockSpec(memory_space=pltpu.VMEM)
    return pl.pallas_call(
        fold_kernel,
        out_shape=jax.ShapeDtypeStruct((parts.shape[2], parts.shape[1]), jnp.float32),
        in_specs=[vmem],
        out_specs=vmem,
        compiler_params=pltpu.CompilerParams(vmem_limit_bytes=16 * 1024 * 1024),
        name="fold",
    )(parts)


def outer_kernel(part_ref, seg_ref, out_ref):
    both = jnp.sum(part_ref[...], axis=0)
    tokens, width = both.shape[0], both.shape[1] // 2
    half = EX_GROUP // 2
    left = both[:, :width]
    col = lax.broadcasted_iota(jnp.int32, (width, width * half), 1)
    row = lax.broadcasted_iota(jnp.int32, (width, width * half), 0)
    repeat = jnp.where(col // half == row, 1.0, 0.0)
    wide = mm(left, repeat, ((1,), (0,)))
    slot = lax.broadcasted_iota(jnp.int32, (tokens, width * half), 1) % half
    seg = seg_ref[...]
    low = jnp.where(slot == seg, wide, 0.0)
    high = jnp.where(slot + half == seg, wide, 0.0)
    lane = lax.broadcasted_iota(jnp.int32, both.shape, 1)
    right = jnp.concatenate([both[:, width:], both[:, width:]], axis=1)
    right_low = jnp.where(lane < width, right, 0.0)
    right_high = jnp.where(lane < width, 0.0, right)
    out = mm(low, right_low, ((0,), (0,))) + mm(high, right_high, ((0,), (0,)))
    out_ref[...] = out.reshape(out_ref.shape)


def outer(parts, seg):
    width = parts.shape[2] // 2
    return pl.pallas_call(
        outer_kernel,
        out_shape=jax.ShapeDtypeStruct((width, EX_GROUP // 2, 2 * width), jnp.float32),
        in_specs=[pl.BlockSpec(memory_space=pltpu.VMEM)] * 2,
        out_specs=pl.BlockSpec(memory_space=pltpu.VMEM),
        compiler_params=pltpu.CompilerParams(vmem_limit_bytes=24 * 1024 * 1024),
        name="outer",
    )(parts, seg)


def per_device(inputs, out_grads, proj_in, proj_out, segment_ids, sketch):
    owners = lax.axis_size(FS)
    blocks = lax.axis_size(XC)
    tokens = inputs.shape[0]
    width = proj_in.shape[1]
    rank = sketch.shape[1]
    half = EX_GROUP // 2
    own_tokens = tokens // owners
    place = lax.axis_index(NEAR + FAR)
    block = lax.axis_index(XC)

    gram = mm(sketch, sketch, ((0,), (0,)))
    upper = [gram[o:o + 128, to:to + 128] for o in range(0, rank, 128) for to in range(o, rank, 128)]
    cut = len(upper) * 128 // blocks
    gram_rows = lax.dynamic_slice_in_dim(jnp.concatenate(upper, axis=0), block * cut, cut, 0)

    segments = segment_ids[0]
    onehot = segments[:, None] == jnp.arange(EX_GROUP, dtype=jnp.int32)[None, :]
    counts = jnp.sum(onehot.astype(jnp.float32), axis=0)
    count_tile = jnp.repeat(counts.reshape(2, half).T, width, axis=1)
    own_segments = lax.dynamic_slice_in_dim(segments, place * own_tokens, own_tokens, 0)[:, None]

    parts = fold(exchange(project(inputs, out_grads, proj_in, proj_out), NEAR))
    parts = exchange(parts.reshape(-1, own_tokens, 2 * width), FAR)
    partial_features = outer(parts, own_segments)
    tile = jnp.sum(exchange(partial_features, FS), axis=0) / count_tile
    tiles = spread(tile, DP)
    sums, features = products(block[None], tiles, sketch, gram_rows)
    chunk = jnp.sum(exchange(sums.reshape(lax.axis_size(NEAR), -1, 128), NEAR), axis=0)
    chunk = jnp.sum(spread(chunk, FAR), axis=0)
    sums = spread(chunk, NEAR).reshape(sums.shape)[: 2 * EX_GROUP * 6 + cut]
    sums = spread(sums, "x")
    other = lax.ppermute(sums, "c", [(0, 1), (1, 0)])
    at = jnp.stack([block * 2 + lax.axis_index("yh"), lax.axis_index("c")])
    return finish(at, sums, other, features, sketch)


def solution(mesh):
    fine = Mesh(mesh.devices.reshape(2, 4, 2, 4, 4, 4), ("yh", "x", "c", "yl", "zh", "zl"))
    return jax.shard_map(
        per_device,
        mesh=fine,
        in_specs=(P(DP, FS), P(DP, FS), P(FS, None), P(FS, None), P(DP, None), P(FS, None)),
        out_specs=(P(FS, None), P(DP, None)),
        check_vma=False,
    )
```

```python
import functools

import jax
import jax.numpy as jnp
from jax import lax
from jax.experimental import pallas as pl
from jax.experimental.pallas import tpu as pltpu
from jax.sharding import Mesh
from jax.sharding import PartitionSpec as P

HI = lax.Precision.HIGHEST
EX_GROUP = 16
DP = ("yh", "x", "c")
XC = ("x", "c")
FS = ("yl", "zh", "zl")
NEAR = ("yl", "zl")
FAR = ("zh",)


def mm(a, b, dims, prec=HI):
    return lax.dot_general(a, b, (dims, ((), ())), precision=prec, preferred_element_type=jnp.float32)

def factor_block(d_ref, w_ref):
    nb = 128
    full = (8, nb)
    lane = lax.broadcasted_iota(jnp.int32, full, 1)
    xs = [d_ref[8 * v: 8 * v + 8, :] for v in range(nb // 8)]
    diag = [jnp.broadcast_to(xs[0][:, j:j + 1], full) for j in range(8)]
    for p in range(nb // 8):
        base = 8 * p
        here = (lane >= base) & (lane < base + 8)
        xr = [jnp.broadcast_to(xs[p][i:i + 1, :], full) for i in range(8)]
        s = [[jnp.broadcast_to(diag[j][i:i + 1, :], full) for j in range(i + 1)] for i in range(8)]
        xr = [jnp.where(here, jnp.where(lane == base + i, 1.0, 0.0), xr[i]) for i in range(8)]
        m = [[None] * 8 for _ in range(8)]
        inv = [None] * 4
        for k in range(0, 8, 2):
            a, b, d = s[k][k], s[k + 1][k], s[k + 1][k + 1]
            det = 1.0 / (a * d - b * b)
            ia, ib, id_ = d * det, b * det, a * det
            inv[k // 2] = (ia, ib, id_)
            for i in range(k + 2, 8):
                m[i][k] = s[i][k] * ia - s[i][k + 1] * ib
                m[i][k + 1] = s[i][k + 1] * id_ - s[i][k] * ib
                for j in range(k + 2, i + 1):
                    s[i][j] = s[i][j] - (m[i][k] * s[j][k] + m[i][k + 1] * s[j][k + 1])
        for i in range(2, 8):
            for k in range(0, i - i % 2, 2):
                xr[i] = xr[i] - (m[i][k] * xr[k] + m[i][k + 1] * xr[k + 1])
        for k in range(0, 8, 2):
            a, b = s[k][k], s[k + 1][k]
            ratio = b / a
            top = xr[k] * lax.rsqrt(a)
            low = (xr[k + 1] - ratio * xr[k]) * lax.rsqrt(s[k + 1][k + 1] - ratio * b)
            w_ref[base + k: base + k + 1, :] = jnp.where(lane < base + 8, top, 0.0)[0:1, :]
            w_ref[base + k + 1: base + k + 2, :] = jnp.where(lane < base + 8, low, 0.0)[0:1, :]
        if p == nb // 8 - 1:
            break
        q = p + 1
        f = [jnp.broadcast_to(xs[q][:, base + i:base + i + 1], full) for i in range(8)]
        diag = [jnp.broadcast_to(xs[q][:, base + 8 + j:base + 9 + j], full) for j in range(8)]
        z = [None] * 8
        for k in range(0, 8, 2):
            ia, ib, id_ = inv[k // 2]
            z[k] = f[k] * ia - f[k + 1] * ib
            z[k + 1] = f[k + 1] * id_ - f[k] * ib
            for i in range(k + 2, 8):
                f[i] = f[i] - (m[i][k] * f[k] + m[i][k + 1] * f[k + 1])
            for j in range(8):
                diag[j] = diag[j] - (
                    z[k] * jnp.broadcast_to(f[k][j:j + 1, :], full)
                    + z[k + 1] * jnp.broadcast_to(f[k + 1][j:j + 1, :], full)
                )
        rest = jnp.where(here, 0.0, xs[q])
        for k in range(0, 8, 2):
            rest = rest - (z[k] * xr[k] + z[k + 1] * xr[k + 1])
        xs[q] = rest
        xv = [None] * 8
        for k in range(6, -1, -2):
            ia, ib, id_ = inv[k // 2]
            xv[k] = xr[k] * ia - xr[k + 1] * ib
            xv[k + 1] = xr[k + 1] * id_ - xr[k] * ib
            for i in range(k + 2, 8):
                xv[k] = xv[k] - m[i][k] * xv[i]
                xv[k + 1] = xv[k + 1] - m[i][k + 1] * xv[i]
        for q in range(p + 2, nb // 8):
            cols = [jnp.broadcast_to(xs[q][:, base + i:base + i + 1], full) for i in range(8)]
            rest = jnp.where(here, 0.0, xs[q])
            xs[q] = rest - (
                ((cols[0] * xv[0] + cols[1] * xv[1]) + (cols[2] * xv[2] + cols[3] * xv[3]))
                + ((cols[4] * xv[4] + cols[5] * xv[5]) + (cols[6] * xv[6] + cols[7] * xv[7]))
            )


def products_kernel(at_ref, tiles_ref, sketch_ref, gram_ref, sums_ref, features_ref):
    groups, half, lanes = tiles_ref.shape
    width = lanes // 2
    for g in range(groups):
        to = ((g % (groups // 2)) * 2 + g // (groups // 2)) * 2 * half
        tile = tiles_ref[g]
        features_ref[to:to + half, :] = tile[:, :width]
        features_ref[to + half:to + 2 * half, :] = tile[:, width:]
    rows = 4 * half
    features = features_ref[...]
    own = features_ref[pl.ds(pl.multiple_of(at_ref[0] * rows, rows), rows), :]
    inner = mm(own, features, ((1,), (1,)))
    scores = mm(own, sketch_ref[...], ((1,), (0,)))
    at = 0
    for part in (inner, scores, gram_ref[...]):
        for o in range(0, part.shape[1], lanes):
            sums_ref[at:at + part.shape[0], :] = part[:, o:o + lanes]
            at += part.shape[0]
    sums_ref[at:, :] = jnp.zeros((sums_ref.shape[0] - at, lanes), jnp.float32)


def products(block, tiles, sketch, gram_rows):
    vmem = pl.BlockSpec(memory_space=pltpu.VMEM)
    return pl.pallas_call(
        products_kernel,
        out_shape=(jax.ShapeDtypeStruct((384, 128), jnp.float32), jax.ShapeDtypeStruct((256, 64), jnp.float32)),
        in_specs=[pl.BlockSpec(memory_space=pltpu.SMEM), vmem, vmem, vmem],
        out_specs=(vmem, vmem),
        compiler_params=pltpu.CompilerParams(vmem_limit_bytes=24 * 1024 * 1024),
        name="products",
    )(block, tiles, sketch, gram_rows)


def finish_kernel(at_ref, sums_ref, sums2_ref, f_ref, s_ref, ns_ref, co_ref, a_ref, x_ref, k_ref, p_ref, g_ref, d_ref, w_ref, wp_ref):
    n = a_ref.shape[0]
    own, e = f_ref.shape[1], f_ref.shape[0]
    across = sums_ref.shape[0]
    rows, cut = e // (2 * across), g_ref.shape[0] // (2 * across)
    for side in range(2):
        core = at_ref[1] if side == 0 else 1 - at_ref[1]
        sums = sums_ref if side == 0 else sums2_ref
        for b in range(across):
            at = 0
            for to, height in ((k_ref, rows), (p_ref, rows), (g_ref, cut)):
                place = pl.ds(pl.multiple_of((2 * b + core) * height, height), height)
                for o in range(0, to.shape[1], 128):
                    to[place, o:o + 128] = sums[b, at:at + height, :]
                    at += height
    k = k_ref[...]
    p = p_ref[...]
    er = lax.broadcasted_iota(jnp.int32, (e, e), 0)
    ec = lax.broadcasted_iota(jnp.int32, (e, e), 1)
    total_sq = jnp.sum(jnp.sum(jnp.where(er == ec, k, 0.0), axis=0, keepdims=True), axis=1, keepdims=True)
    c = 16.0 / (total_sq + 1e-6)
    q = p + mm(k * c, p, ((1,), (0,)))
    pq = p + q
    pc = p * c
    colid = lax.broadcasted_iota(jnp.int32, (128, n), 1)

    def next_block(o, t):
        w = w_ref[...]
        wp_ref[...] = w
        r = mm(w, a_ref[pl.ds(o, 128), pl.ds(t, 128)], ((1,), (0,)))
        d_ref[...] = a_ref[pl.ds(t, 128), pl.ds(t, 128)] - mm(r, r, ((0,), (0,)))

    d_ref[...] = g_ref[:128, :] + mm(pc[:, :128], pq[:, :128], ((0,), (0,)))
    x_ref[:own, :] = s_ref[...] + mm(f_ref[...] * c, p, ((0,), (0,)))
    x_ref[own:, :] = q
    at = 0
    for o in range(0, n, 128):
        update = mm(pc[:, o:o + 128], pq[:, o:], ((0,), (0,)))
        if o > 0:
            a_ref[o:o + 128, :o] = jnp.zeros((128, o), jnp.float32)
        for to in range(o, n, 128):
            a_ref[o:o + 128, to:to + 128] = g_ref[at:at + 128, :] + update[:, to - o:to - o + 128]
            at += 128
    factor_block(d_ref, w_ref)
    next_block(0, 128)

    def step(b, carry):
        o = pl.multiple_of(b * 128, 128)
        before = pl.multiple_of(o - 128, 128)
        wp = wp_ref[...]
        r = jnp.where(colid >= o, mm(wp, a_ref[pl.ds(before, 128), :], ((1,), (0,))), 0.0)
        y = mm(x_ref[:, pl.ds(before, 128)], wp, ((1,), (1,)))
        x_ref[:, pl.ds(before, 128)] = y
        x_ref[...] = x_ref[...] - mm(y, r, ((1,), (0,)))
        a_ref[...] = a_ref[...] - mm(r, r, ((0,), (0,)))
        factor_block(d_ref, w_ref)
        next_block(o, pl.multiple_of(jnp.minimum(o + 128, n - 128), 128))
        return carry

    lax.fori_loop(1, n // 128, step, 0)
    x_ref[:, n - 128:] = mm(x_ref[:, n - 128:], wp_ref[...], ((1,), (1,)))
    ns_ref[...] = x_ref[:own, :]
    coefs = x_ref[own:, :]
    mean = jnp.sum(coefs * coefs, axis=0, keepdims=True) / e
    mine = x_ref[pl.ds(pl.multiple_of(own + at_ref[0] * EX_GROUP, EX_GROUP), EX_GROUP), :]
    co_ref[...] = mine / jnp.sqrt(mean + 1e-6)


def finish(at, sums, sums2, f, s):
    n, own, e = s.shape[1], s.shape[0], f.shape[0]
    vmem = pl.BlockSpec(memory_space=pltpu.VMEM)
    return pl.pallas_call(
        finish_kernel,
        out_shape=(jax.ShapeDtypeStruct((own, n), jnp.float32), jax.ShapeDtypeStruct((EX_GROUP, n), jnp.float32)),
        in_specs=[pl.BlockSpec(memory_space=pltpu.SMEM)] + [vmem] * 4,
        out_specs=(vmem, vmem),
        scratch_shapes=[
            pltpu.VMEM((n, n), jnp.float32),
            pltpu.VMEM((own + e, n), jnp.float32),
            pltpu.VMEM((e, e), jnp.float32),
            pltpu.VMEM((e, n), jnp.float32),
            pltpu.VMEM((n * (n + 128) // 256, 128), jnp.float32),
            pltpu.VMEM((128, 128), jnp.float32),
            pltpu.VMEM((128, 128), jnp.float32),
            pltpu.VMEM((128, 128), jnp.float32),
        ],
        compiler_params=pltpu.CompilerParams(vmem_limit_bytes=40 * 1024 * 1024),
        name="finish",
    )(at, sums, sums2, f, s)


def exchange(x, axes):
    return lax.all_to_all(x, axes, 0, 0, tiled=True)


def spread(x, axes):
    return exchange(jnp.broadcast_to(x[None], (lax.axis_size(axes),) + x.shape), axes)


def project_kernel(x_ref, y_ref, px_ref, py_ref, out_ref):
    left = lax.dot_general(px_ref[...], x_ref[...], (((1,), (1,)), ((), ())), preferred_element_type=jnp.float32)
    right = lax.dot_general(py_ref[...], y_ref[...], (((1,), (0,)), ((), ())), preferred_element_type=jnp.float32)
    width = left.shape[0]
    for c in range(out_ref.shape[0]):
        out_ref[c, :width, :] = left[:, c * 128:(c + 1) * 128]
        out_ref[c, width:, :] = right[:, c * 128:(c + 1) * 128]


def project(x, y, px, py):
    tokens, width = x.shape[0], px.shape[1]
    step = tokens // 2
    return pl.pallas_call(
        project_kernel,
        grid=(2,),
        out_shape=jax.ShapeDtypeStruct((tokens // 128, 2 * width, 128), jnp.float32),
        in_specs=[
            pl.BlockSpec((step, x.shape[1]), lambda i: (i, 0)),
            pl.BlockSpec((y.shape[1], step), lambda i: (0, i)),
            pl.BlockSpec((width, x.shape[1]), lambda i: (0, 0)),
            pl.BlockSpec((width, y.shape[1]), lambda i: (0, 0)),
        ],
        out_specs=pl.BlockSpec((step // 128, 2 * width, 128), lambda i: (i, 0, 0)),
        name="project",
    )(x, y.T, px.T, py.T)


def fold_kernel(parts_ref, out_ref):
    out_ref[...] = jnp.sum(parts_ref[...], axis=0).T


def fold(parts):
    vmem = pl.BlockSpec(memory_space=pltpu.VMEM)
    return pl.pallas_call(
        fold_kernel,
        out_shape=jax.ShapeDtypeStruct((parts.shape[2], parts.shape[1]), jnp.float32),
        in_specs=[vmem],
        out_specs=vmem,
        compiler_params=pltpu.CompilerParams(vmem_limit_bytes=16 * 1024 * 1024),
        name="fold",
    )(parts)


def outer_kernel(part_ref, seg_ref, out_ref):
    both = jnp.sum(part_ref[...], axis=0)
    tokens, width = both.shape[0], both.shape[1] // 2
    half = EX_GROUP // 2
    left = both[:, :width]
    col = lax.broadcasted_iota(jnp.int32, (width, width * half), 1)
    row = lax.broadcasted_iota(jnp.int32, (width, width * half), 0)
    repeat = jnp.where(col // half == row, 1.0, 0.0)
    wide = mm(left, repeat, ((1,), (0,)))
    slot = lax.broadcasted_iota(jnp.int32, (tokens, width * half), 1) % half
    seg = seg_ref[...]
    low = jnp.where(slot == seg, wide, 0.0)
    high = jnp.where(slot + half == seg, wide, 0.0)
    lane = lax.broadcasted_iota(jnp.int32, both.shape, 1)
    right = jnp.concatenate([both[:, width:], both[:, width:]], axis=1)
    right_low = jnp.where(lane < width, right, 0.0)
    right_high = jnp.where(lane < width, 0.0, right)
    out = mm(low, right_low, ((0,), (0,))) + mm(high, right_high, ((0,), (0,)))
    out_ref[...] = out.reshape(out_ref.shape)


def outer(parts, seg):
    width = parts.shape[2] // 2
    return pl.pallas_call(
        outer_kernel,
        out_shape=jax.ShapeDtypeStruct((width, EX_GROUP // 2, 2 * width), jnp.float32),
        in_specs=[pl.BlockSpec(memory_space=pltpu.VMEM)] * 2,
        out_specs=pl.BlockSpec(memory_space=pltpu.VMEM),
        compiler_params=pltpu.CompilerParams(vmem_limit_bytes=24 * 1024 * 1024),
        name="outer",
    )(parts, seg)


def per_device(inputs, out_grads, proj_in, proj_out, segment_ids, sketch):
    owners = lax.axis_size(FS)
    blocks = lax.axis_size(XC)
    tokens = inputs.shape[0]
    width = proj_in.shape[1]
    rank = sketch.shape[1]
    half = EX_GROUP // 2
    own_tokens = tokens // owners
    place = lax.axis_index(NEAR + FAR)
    block = lax.axis_index(XC)

    gram = mm(sketch, sketch, ((0,), (0,)))
    upper = [gram[o:o + 128, to:to + 128] for o in range(0, rank, 128) for to in range(o, rank, 128)]
    cut = len(upper) * 128 // blocks
    gram_rows = lax.dynamic_slice_in_dim(jnp.concatenate(upper, axis=0), block * cut, cut, 0)

    segments = segment_ids[0]
    onehot = segments[:, None] == jnp.arange(EX_GROUP, dtype=jnp.int32)[None, :]
    counts = jnp.sum(onehot.astype(jnp.float32), axis=0)
    count_tile = jnp.repeat(counts.reshape(2, half).T, width, axis=1)
    own_segments = lax.dynamic_slice_in_dim(segments, place * own_tokens, own_tokens, 0)[:, None]

    parts = fold(exchange(project(inputs, out_grads, proj_in, proj_out), NEAR))
    parts = exchange(parts.reshape(-1, own_tokens, 2 * width), FAR)
    partial_features = outer(parts, own_segments)
    tile = jnp.sum(exchange(partial_features, FS), axis=0) / count_tile
    tiles = spread(tile, DP)
    sums, features = products(block[None], tiles, sketch, gram_rows)
    chunk = jnp.sum(exchange(sums.reshape(lax.axis_size(NEAR), -1, 128), NEAR), axis=0)
    chunk = jnp.sum(spread(chunk, FAR), axis=0)
    sums = spread(chunk, NEAR).reshape(sums.shape)[: 2 * EX_GROUP * 6 + cut]
    sums = spread(sums, "x")
    other = lax.ppermute(sums, "c", [(0, 1), (1, 0)])
    at = jnp.stack([block * 2 + lax.axis_index("yh"), lax.axis_index("c")])
    return finish(at, sums, other, features, sketch)


def solution(mesh):
    fine = Mesh(mesh.devices.reshape(2, 4, 2, 4, 4, 4), ("yh", "x", "c", "yl", "zh", "zl"))
    return jax.shard_map(
        per_device,
        mesh=fine,
        in_specs=(P(DP, FS), P(DP, FS), P(FS, None), P(FS, None), P(DP, None), P(FS, None)),
        out_specs=(P(FS, None), P(DP, None)),
        check_vma=False,
    )
```
